128 devices in a mesh: row: 16 (over z_lo, x, core), col: 8 (over z_hi, y).
Axes of the slice: x: 4, y: 4, z: 4 (z_hi: 2, z_lo: 2; z = z_hi * 2 + z_lo), core: 2. Of those that a mesh axis runs over, the one named last changes fastest.
Arguments:
- inverse_front: float32 [16384, 16384], P('row', 'col'), may hold values from -0.09375 to 0.09375
- factor: float32 [4096, 1024], P('row'), may hold values from -1.2 to 1.2
- unit_lower: float32 [2, 512, 512], replicated, may hold values from -0.25 to 0.25
- pivot_inverse: float32 [2, 512], replicated, may hold values from 0.5 to 4
- tile_list: int32 [2, 16], replicated, may hold values from 0 to 63, as said below
- tile_valid: int32 [2, 16], replicated, may hold values from 0 to 1, as said below
Outputs:
- inverse_column: float32 [16384, 1024], P('row')
- diagonal_block: float32 [2, 512, 512], replicated
The draws below stay inside these ranges and needn't reach their ends.
Inputs may be any that keep to these rules, and one draw needn't show every extreme that they name: `tile_list`: each row names 16 different tile rows of the front in increasing order, exactly 1 of them among each aligned group of 4 tile rows, and the last tile row is always among them. `tile_valid`: each row holds at least one 1.
All inputs are finite; a program needn't handle non-finite values.
Results may differ from the reference program's by a relative error of at most 0.0001.
Values sent between devices are 32-bit elements; how exact they have to be, the bound alone decides.
A program may use at most 192 MiB of HBM per device.

```python
import math
import jax
import jax.numpy as jnp
from jax import lax

F = 16384
B = 256
W = 512
NS = 2
NA = 16
R = 4096
N_ROW = 16


def draw_tile_list(key, part):
    group_tiles = F // (B * N_ROW)
    picks = NA // N_ROW
    local = jnp.arange(group_tiles, dtype=jnp.int32)
    noise = jax.random.randint(jax.random.fold_in(key, 11), (NS, N_ROW, group_tiles), 0, 1000, dtype=jnp.int32)
    scores = noise * group_tiles + local[None, None, :]
    last_group = jnp.arange(N_ROW, dtype=jnp.int32)[None, :, None] == N_ROW - 1
    last_tile = local[None, None, :] == group_tiles - 1
    scores = jnp.where(last_group & last_tile, 4000 * group_tiles, scores)
    picked = lax.top_k(scores, picks)[1]
    picked = jnp.sort(picked, axis=2)
    base = (jnp.arange(N_ROW, dtype=jnp.int32) * group_tiles)[None, :, None]
    return (picked + base).reshape(NS, NA).astype(jnp.int32)


def draw_tile_valid(key, part):
    mask = jax.random.randint(jax.random.fold_in(key, 21), (NS, NA), 0, 4, dtype=jnp.int32) < 3
    forced = jax.random.randint(jax.random.fold_in(key, 22), (NS, 1), 0, NA, dtype=jnp.int32)
    slot = jnp.arange(NA, dtype=jnp.int32)[None, :]
    return (mask | (slot == forced)).astype(jnp.int32)


def block_levels(stream_key, extent, split, low, largest):
    level, own = 1.0, jax.random.fold_in(stream_key, 6)
    for dim, blocks in split:
        draws = jnp.exp(jax.random.uniform(jax.random.fold_in(own, dim), (blocks,), jnp.float32, low / len(split), largest / len(split)))
        level = level * jnp.repeat(draws, extent[dim] // blocks).reshape([-1 if axis == dim else 1 for axis in range(len(extent))])
    return level


def centred(stream_key, shape, width, reach, shards=(), kind=jnp.bfloat16):
    level = block_levels(stream_key, shape, shards, -0.22, 0.18) if shards else 1.0
    entries = jax.random.normal(stream_key, shape, jnp.float32) * width * level
    return jnp.minimum(jnp.maximum(entries, -reach), reach).astype(kind)


def setup_inputs(seed: int = 0) -> dict:
    arg_keys = jax.random.split(jax.random.key(seed), 7)
    return {
        "inverse_front": centred(arg_keys[0], (F, F), (NA * B) ** -0.5, 0.09375, ((0, 16), (1, 8)), jnp.float32),
        "factor": centred(arg_keys[1], (R, NS * W), 0.2, 1.2, ((0, 16),), jnp.float32),
        "unit_lower": centred(arg_keys[2], (NS, W, W), W ** -0.5, 0.25, (), jnp.float32),
        "pivot_inverse": jnp.clip(jnp.exp(jax.random.uniform(arg_keys[3], (NS, W), jnp.float32, math.log(0.5), math.log(4.0))), 0.5, 4.0),
        "tile_list": draw_tile_list(jax.random.fold_in(arg_keys[6], 71), 0),
        "tile_valid": draw_tile_valid(jax.random.fold_in(arg_keys[6], 71), 0),
    }


def reference(inverse_front, factor, unit_lower, pivot_inverse, tile_list, tile_valid):
    identity = jnp.eye(W, dtype=jnp.float32)
    result = jnp.zeros((F, NS * W), jnp.float32)
    blocks = []
    for member in range(NS):
        inverse_s = jnp.tril(unit_lower[member], -1) + identity
        slab = factor[:, member * W:(member + 1) * W]
        normalized = jnp.dot(slab, inverse_s, precision=lax.Precision.HIGHEST, preferred_element_type=jnp.float32)
        row_keep = jnp.repeat(tile_valid[member].astype(jnp.float32), B)
        normalized = normalized * row_keep[:, None]
        row_global = (tile_list[member][:, None] * B + jnp.arange(B, dtype=jnp.int32)[None, :]).reshape(-1).astype(jnp.int32)
        picked_rows = jnp.take(inverse_front, row_global, axis=0)
        gathered = jnp.take(picked_rows, row_global, axis=1)
        symmetric = jnp.where(row_global[:, None] >= row_global[None, :], gathered, gathered.T)
        column = -jnp.dot(symmetric, normalized, precision=lax.Precision.HIGHEST, preferred_element_type=jnp.float32)
        column = column * row_keep[:, None]
        result = result.at[row_global, member * W:(member + 1) * W].set(column)
        base_block = jnp.dot(inverse_s.T * pivot_inverse[member][None, :], inverse_s, precision=lax.Precision.HIGHEST, preferred_element_type=jnp.float32)
        update = jnp.dot(normalized.T, column, precision=lax.Precision.HIGHEST, preferred_element_type=jnp.float32)
        blocks.append(base_block - update)
    return result, jnp.stack(blocks)
```

```python
import jax
import jax.numpy as jnp
from jax import lax
from jax.experimental import pallas as pl
from jax.experimental.pallas import tpu as pltpu
from jax.sharding import PartitionSpec as P

B = 256
W = 512
NS = 2
NA = 16
NC = 8
LANES = 128
PIECE = W // NA
MESH = pl.DeviceIdType.MESH
F32 = jnp.float32
BF16 = jnp.bfloat16


def split(x):
    hi = x.astype(BF16)
    return hi, (x - hi.astype(F32)).astype(BF16)


def mm(a, b, dims=(1, 0)):
    def dot(x, y):
        return lax.dot_general(x, y, (((dims[0],), (dims[1],)), ((), ())), preferred_element_type=F32)

    return dot(a[0], b[0]) + (dot(a[0], b[1]) + dot(a[1], b[0]))


def prepare(tile_list, tile_valid, front, factor, lower, pivot, tiles_out, norm_out, base_out, sems):
    r = lax.axis_index("row")
    c = lax.axis_index("col")
    copies = []
    for s in range(NS):
        for j in range(2):
            row = (tile_list[s, r] - 4 * r) * B
            col = (tile_list[s, 2 * c + j] - 8 * c) * B
            src = front.at[pl.ds(pl.multiple_of(row, B), B), pl.ds(pl.multiple_of(col, B), B)]
            copies.append(pltpu.make_async_copy(src, tiles_out.at[2 * s + j], sems.at[2 * s + j]))
    for copy in copies:
        copy.start()
    i0 = lax.broadcasted_iota(jnp.int32, (W, W), 0)
    i1 = lax.broadcasted_iota(jnp.int32, (W, W), 1)
    for s in range(NS):
        inv = jnp.where(i0 > i1, lower[s], jnp.where(i0 == i1, 1.0, 0.0))
        keep = (tile_valid[s, r] > 0).astype(F32)
        fac = factor[:, s * W : (s + 1) * W] * keep
        inv_split = split(inv)
        norm_out[s] = mm(split(fac), inv_split)

        @pl.when(c // 4 == s)
        def _():
            i2 = lax.broadcasted_iota(jnp.int32, (W, LANES), 0)
            i3 = lax.broadcasted_iota(jnp.int32, (W, LANES), 1) + (c % 4) * LANES
            lanes = pl.ds(pl.multiple_of((c % 4) * LANES, LANES), LANES)
            part = jnp.where(i2 > i3, lower[s, :, lanes], jnp.where(i2 == i3, 1.0, 0.0))
            scaled = part * pivot[s].T
            base_out[...] = mm(inv_split, split(scaled), (0, 0))

    for copy in copies:
        copy.wait()
    own = r - 2 * c
    b0 = lax.broadcasted_iota(jnp.int32, (B, B), 0)
    b1 = lax.broadcasted_iota(jnp.int32, (B, B), 1)
    for j in range(2):

        @pl.when(own == j)
        def _():
            for s in range(NS):
                tile = tiles_out[2 * s + j]
                tiles_out[2 * s + j] = jnp.where(b0 >= b1, tile, tile.T)


def exchange(
    tiles, norm, base, c_all, d_all,
    st, nr, q_loc, q_rx, p_out, q_out, c_rx, d_part, d_rx,
    st_s, st_r, n_s, n_r, g_s, g_r, q_s, q_r, p_ss, q_ss, c_r, ca_s, ca_r, dp_s, dp_r, da_s, da_r, db_s, db_r, dc_s, dc_r,
):
    r = lax.axis_index("row")
    c = lax.axis_index("col")
    k = r // 2
    q = r % 2
    cy = c % 4
    cz = c // 4
    sib = (r + 1 - 2 * q, c)
    lower = k > c
    upper = k < c
    off = k != c
    diag = k == c
    s_own = jnp.where(lower, 0, 1)
    pending = []

    def copy(src, dst, ssem, rsem, dev):
        return pltpu.make_async_remote_copy(
            src_ref=src, dst_ref=dst, send_sem=ssem, recv_sem=rsem, device_id=dev, device_id_type=MESH
        )

    def send(cond, make):
        pl.when(cond)(lambda: make().start())
        pending.append((cond, make))

    def arrived(buf, sem):
        copy(buf, buf, sem, sem, sib).wait_recv()

    for j in range(2):
        send(lower, lambda j=j: copy(tiles.at[2 + j], st.at[q], st_s.at[j], st_r.at[q], (2 * c + j, k)))
    send(off, lambda: copy(norm.at[1 - s_own], nr.at[q], n_s.at[0], n_r.at[q], (2 * c + q, k)))
    send(diag & (q == 0), lambda: copy(norm, nr, g_s.at[0], g_r.at[2], sib))

    def ship(slices, sems, s, row, slot):
        for d in range(4):
            def make(d=d):
                return copy(slices.at[d], c_rx.at[slot], sems.at[d], c_r.at[slot], (row, 4 * s + d))
            yield d, make

    def send_slices(cond, slices, sems, s, row, slot):
        for d, make in ship(slices, sems, s, row, slot):
            mine = (row == r) & (4 * s + d == c)
            send(cond & jnp.logical_not(mine), make)

            @pl.when(cond & mine)
            def _():
                c_rx[slot] = slices[d]

    n_own = norm.at[s_own]

    @pl.when(off)
    def _():
        own = split(n_own[...])
        for j in range(2):

            @pl.when(lower)
            def _():
                q_loc[j] = mm(split(tiles[j]), own, (0, 0))

            @pl.when(upper)
            def _():
                arrived(st.at[j], st_r.at[j])
                q_loc[j] = mm(split(st[j]), own)

    send(off, lambda: copy(q_loc.at[1 - q], q_rx.at[0], q_s.at[0], q_r.at[0], sib))

    @pl.when(off)
    def _():
        arrived(nr.at[q], n_r.at[q])

    send(off, lambda: copy(nr.at[q], nr.at[q], g_s.at[1], g_r.at[q], sib))

    @pl.when(off)
    def _():
        arrived(q_rx.at[0], q_r.at[0])
        for d in range(4):
            lanes = slice(d * LANES, (d + 1) * LANES)
            q_out[d] = q_loc[q, :, lanes] + q_rx[0, :, lanes]

    send_slices(off, q_out, q_ss, s_own, 2 * c + q, k)

    @pl.when(off)
    def _():
        arrived(nr.at[1 - q], g_r.at[1 - q])

        def put(value):
            for d in range(4):
                p_out[0, d] = value[:, d * LANES : (d + 1) * LANES]

        @pl.when(lower)
        def _():
            put(mm(split(tiles[0]), split(nr[0])) + mm(split(tiles[1]), split(nr[1])))

        @pl.when(upper)
        def _():
            put(mm(split(st[0]), split(nr[0]), (0, 0)) + mm(split(st[1]), split(nr[1]), (0, 0)))

    @pl.when(diag & (q == 1))
    def _():
        for s in range(NS):
            q_loc[s] = mm(split(tiles[2 * s]), split(norm[s]), (0, 0))

    for s in range(NS):
        send(diag & (q == 1), lambda s=s: copy(q_loc.at[s], q_rx.at[s], q_s.at[1 + s], q_r.at[1 + s], sib))

    @pl.when(diag & (q == 1))
    def _():
        arrived(nr, g_r.at[2])
        for s in range(NS):
            value = mm(split(tiles[2 * s]), split(nr[s])) + mm(split(tiles[2 * s + 1]), split(norm[s]))
            for d in range(4):
                p_out[s, d] = value[:, d * LANES : (d + 1) * LANES]

    @pl.when(diag & (q == 0))
    def _():
        for s in range(NS):
            value = mm(split(tiles[2 * s]), split(norm[s]))
            arrived(q_rx.at[s], q_r.at[1 + s])
            for d in range(4):
                lanes = slice(d * LANES, (d + 1) * LANES)
                p_out[s, d] = value[:, lanes] + q_rx[s, :, lanes]

    send_slices(off, p_out.at[0], p_ss.at[0], s_own, r, c)
    for s in range(NS):
        send_slices(diag, p_out.at[s], p_ss.at[s], s, r, c)

    own_slot = diag | (lower & (c < 4)) | (upper & (c >= 4))
    total = None
    for m in range(NC):

        @pl.when(jnp.logical_not(own_slot & (c == m)))
        def _():
            arrived(c_rx.at[m], c_r.at[m])

        total = c_rx[m] if total is None else total + c_rx[m]
    column = -total
    c_all[c] = column
    for d in range(1, NC):
        to = (c + d) % NC
        send(True, lambda d=d, to=to: copy(c_all.at[c], c_all.at[c], ca_s.at[d], ca_r.at[c], (r, to)))

    part = mm(split(norm[cz]), split(column), (0, 0))
    for a in range(NA):
        d_part[a] = part[a * PIECE : (a + 1) * PIECE]
    for d in range(1, NA):
        to = (r + d) % NA
        send(True, lambda d=d, to=to: copy(d_part.at[to], d_rx.at[r], dp_s.at[d], dp_r.at[r], (to, c)))
    acc = base[pl.ds(pl.multiple_of(r * PIECE, PIECE), PIECE), :] - d_part[r]
    for d in range(1, NA):
        of = (r + d) % NA
        arrived(d_rx.at[of], dp_r.at[of])
        acc = acc - d_rx[of]
    d_all[r, c] = acc
    for d in range(1, NC):
        to = (c + d) % NC
        send(True, lambda d=d, to=to: copy(d_all.at[r, c], d_all.at[r, c], da_s.at[d], da_r.at[c], (r, to)))
    for d in range(1, NC):
        of = (c + d) % NC
        arrived(d_all.at[r, of], da_r.at[of])
    for d in range(1, NC):
        to = (r + 2 * d) % NA
        send(True, lambda d=d, to=to: copy(d_all.at[r], d_all.at[r], db_s.at[d], db_r.at[k], (to, c)))
    send(True, lambda: copy(d_all.at[r], d_all.at[r], dc_s.at[0], dc_r.at[k], sib))
    for d in range(1, NC):
        of = (r + 2 * d) % NA
        arrived(d_all.at[of], db_r.at[of // 2])
        send(True, lambda d=d, of=of: copy(d_all.at[of], d_all.at[of], dc_s.at[d], dc_r.at[of // 2], sib))
    for m in range(NC):
        arrived(d_all.at[2 * m + 1 - q], dc_r.at[m])
    for d in range(1, NC):
        of = (c + d) % NC
        arrived(c_all.at[of], ca_r.at[of])
    for cond, make in pending:
        pl.when(cond)(lambda make=make: make().wait_send())


def place(tile_list, tile_valid, c_all, d_all, column_out, diag_out):
    t = pl.program_id(0)
    r = lax.axis_index("row")
    for s in range(NS):
        here = (tile_list[s, r] == 4 * r + t) & (tile_valid[s, r] > 0)
        for j in range(4):
            lanes = slice((4 * s + j) * LANES, (4 * s + j + 1) * LANES)
            column_out[:, lanes] = jnp.where(here, c_all[4 * s + j], 0.0)
            for a in range(4):
                diag_out[s, a * PIECE : (a + 1) * PIECE, j * LANES : (j + 1) * LANES] = d_all[a, 4 * s + j]


def shards(inverse_front, factor, unit_lower, pivot_inverse, tile_list, tile_valid):
    smem = pl.BlockSpec(memory_space=pltpu.SMEM)
    vmem = pl.BlockSpec(memory_space=pltpu.VMEM)
    tiles, norm, base = pl.pallas_call(
        prepare,
        out_shape=(
            jax.ShapeDtypeStruct((4, B, B), F32),
            jax.ShapeDtypeStruct((NS, B, W), F32),
            jax.ShapeDtypeStruct((W, LANES), F32),
        ),
        in_specs=[smem, smem, pl.BlockSpec(memory_space=pl.ANY), vmem, vmem, vmem],
        out_specs=(vmem, vmem, vmem),
        scratch_shapes=[pltpu.SemaphoreType.DMA((4,))],
        name="prepare",
    )(tile_list, tile_valid, inverse_front, factor, unit_lower, pivot_inverse.reshape(NS, 1, W))

    dma = pltpu.SemaphoreType.DMA
    c_all, d_all = pl.pallas_call(
        exchange,
        out_shape=(
            jax.ShapeDtypeStruct((NC, B, LANES), F32),
            jax.ShapeDtypeStruct((NA, NC, PIECE, LANES), F32),
        ),
        in_specs=[vmem, vmem, vmem],
        out_specs=(vmem, vmem),
        scratch_shapes=[
            pltpu.VMEM((2, B, B), F32),
            pltpu.VMEM((2, B, W), F32),
            pltpu.VMEM((2, B, W), F32),
            pltpu.VMEM((2, B, W), F32),
            pltpu.VMEM((2, 4, B, LANES), F32),
            pltpu.VMEM((4, B, LANES), F32),
            pltpu.VMEM((NC, B, LANES), F32),
            pltpu.VMEM((NA, PIECE, LANES), F32),
            pltpu.VMEM((NA, PIECE, LANES), F32),
            dma((2,)), dma((2,)),
            dma((1,)), dma((2,)),
            dma((2,)), dma((3,)),
            dma((3,)), dma((3,)),
            dma((2, 4)), dma((4,)), dma((NC,)),
            dma((NC,)), dma((NC,)),
            dma((NA,)), dma((NA,)),
            dma((NC,)), dma((NC,)),
            dma((NC,)), dma((NC,)),
            dma((NC,)), dma((NC,)),
        ],
        compiler_params=pltpu.CompilerParams(has_side_effects=True),
        name="exchange",
    )(tiles, norm, base)

    whole = lambda shape: pl.BlockSpec(shape, lambda t: (0,) * len(shape))
    return pl.pallas_call(
        place,
        grid=(4,),
        out_shape=(
            jax.ShapeDtypeStruct((4 * B, NS * W), F32),
            jax.ShapeDtypeStruct((NS, W, W), F32),
        ),
        in_specs=[
            smem,
            smem,
            whole((NC, B, LANES)),
            pl.BlockSpec((4, NC, PIECE, LANES), lambda t: (t, 0, 0, 0)),
        ],
        out_specs=(
            pl.BlockSpec((B, NS * W), lambda t: (t, 0)),
            pl.BlockSpec((NS, W // 4, W), lambda t: (0, t, 0)),
        ),
        name="place",
    )(tile_list, tile_valid, c_all, d_all)


def solution(mesh):
    in_specs = (P("row", "col"), P("row", None), P(), P(), P(), P())
    out_specs = (P("row", None), P())
    return jax.shard_map(shards, mesh=mesh, in_specs=in_specs, out_specs=out_specs, check_vma=False)
```

```python
import jax
import jax.numpy as jnp
from jax import lax
from jax.experimental import pallas as pl
from jax.experimental.pallas import tpu as pltpu
from jax.sharding import PartitionSpec as P

B = 256
W = 512
NS = 2
NA = 16
NC = 8
LANES = 128
PIECE = W // NA
MESH = pl.DeviceIdType.MESH
F32 = jnp.float32
BF16 = jnp.bfloat16


def split(x):
    hi = x.astype(BF16)
    return hi, (x - hi.astype(F32)).astype(BF16)


def mm(a, b, dims=(1, 0)):
    def dot(x, y):
        return lax.dot_general(x, y, (((dims[0],), (dims[1],)), ((), ())), preferred_element_type=F32)

    return dot(a[0], b[0]) + (dot(a[0], b[1]) + dot(a[1], b[0]))


def prepare(tile_list, tile_valid, front, factor, lower, pivot, tiles_out, norm_out, base_out, sems):
    r = lax.axis_index("row")
    c = lax.axis_index("col")
    copies = []
    for s in range(NS):
        for j in range(2):
            row = (tile_list[s, r] - 4 * r) * B
            col = (tile_list[s, 2 * c + j] - 8 * c) * B
            src = front.at[pl.ds(pl.multiple_of(row, B), B), pl.ds(pl.multiple_of(col, B), B)]
            copies.append(pltpu.make_async_copy(src, tiles_out.at[2 * s + j], sems.at[2 * s + j]))
    for copy in copies:
        copy.start()
    i0 = lax.broadcasted_iota(jnp.int32, (W, W), 0)
    i1 = lax.broadcasted_iota(jnp.int32, (W, W), 1)
    for s in range(NS):
        inv = jnp.where(i0 > i1, lower[s], jnp.where(i0 == i1, 1.0, 0.0))
        keep = (tile_valid[s, r] > 0).astype(F32)
        fac = factor[:, s * W : (s + 1) * W] * keep
        inv_split = split(inv)
        norm_out[s] = mm(split(fac), inv_split)

        @pl.when(c // 4 == s)
        def _():
            i2 = lax.broadcasted_iota(jnp.int32, (W, LANES), 0)
            i3 = lax.broadcasted_iota(jnp.int32, (W, LANES), 1) + (c % 4) * LANES
            lanes = pl.ds(pl.multiple_of((c % 4) * LANES, LANES), LANES)
            part = jnp.where(i2 > i3, lower[s, :, lanes], jnp.where(i2 == i3, 1.0, 0.0))
            scaled = part * pivot[s].T
            base_out[...] = mm(inv_split, split(scaled), (0, 0))

    for copy in copies:
        copy.wait()
    own = r - 2 * c
    b0 = lax.broadcasted_iota(jnp.int32, (B, B), 0)
    b1 = lax.broadcasted_iota(jnp.int32, (B, B), 1)
    for j in range(2):

        @pl.when(own == j)
        def _():
            for s in range(NS):
                tile = tiles_out[2 * s + j]
                tiles_out[2 * s + j] = jnp.where(b0 >= b1, tile, tile.T)


FULL = (
    ((0, 1), (0, 1), (0, 0), (0, 0)),
    ((0, 1), (1, 1), (0, 0), (0, 0)),
    ((1, 0), (3, 1), (2, 0), (0, 1)),
    ((2, 1), (0, 0), (1, 1), (1, 0)),
)
PAIRS0 = (
    (1, 0, ((1, 0), (3, 0), (2, 0), (2, 1))),
    (2, 0, ((2, 0), (1, 1), (3, 0), (0, 1))),
    (3, 0, ((0, 0), (1, 0), (3, 0), (3, 1))),
    (2, 1, ((2, 0), (3, 0), (2, 1), (1, 0))),
    (3, 1, ((2, 0), (1, 1), (3, 1), (3, 0))),
    (3, 2, ((3, 1), (1, 0), (3, 0), (3, 0))),
)
PAIRS3 = (
    (1, 0, ((1, 1), (0, 1), (3, 1), (2, 1))),
    (2, 0, ((2, 1), (1, 0), (1, 1), (0, 1))),
    (3, 0, ((3, 1), (0, 0), (1, 1), (3, 0))),
    (2, 1, ((0, 1), (3, 0), (2, 0), (2, 1))),
    (3, 1, ((1, 1), (2, 1), (3, 1), (1, 0))),
    (3, 2, ((0, 1), (2, 0), (3, 1), (1, 1))),
)
HALF = B // 2


def exchange(
    tiles, norm, base, c_all, d_all,
    nr, q_loc, q_rx, p_out, q_out, cp_rx, cq_rx, p_sum, q_sum, pf_rx, qt_rx, d_part, d_rx,
    n_s, n_r, g_s, g_r, q_s, q_r, p_ss, q_ss, cp_r, cq_r, f_s, f_r, t_s, t_r,
    ca_s, ca_r, dp_s, dp_r, da_s, da_r, db_s, db_r, dc_s, dc_r,
):
    r = lax.axis_index("row")
    c = lax.axis_index("col")
    k = r // 2
    q = r % 2
    x = k % 4
    zl = k // 4
    y = cy = c % 4
    zh = cz = c // 4
    sib = (r + 1 - 2 * q, c)
    lower = k > c
    diag = k == c
    full = (zl == 1) & (zh == 0)
    tri = zl == zh
    work = full | tri
    pending = []

    def copy(src, dst, ssem, rsem, dev):
        return pltpu.make_async_remote_copy(
            src_ref=src, dst_ref=dst, send_sem=ssem, recv_sem=rsem, device_id=dev, device_id_type=MESH
        )

    def send(cond, make):
        pl.when(cond)(lambda: make().start())
        pending.append((cond, make))

    def arrived(buf, sem):
        copy(buf, buf, sem, sem, sib).wait_recv()

    def give(cond, j, sem, row, col):
        part = pl.ds(j % 2 * HALF, HALF)
        send(cond, lambda: copy(norm.at[j // 2, part], nr.at[q, j // 2, part], n_s.at[sem], n_r.at[j], (row, col)))

    count = 0
    for j in range(4):
        for d in range(4):
            alpha, side = FULL[d][j]
            give((zl == 0) & (zh == side) & ((y - x + 4) % 4 == alpha), j, count, 8 + 2 * ((x + d) % 4) + q, x)
            count += 1
        for n, pairs in ((0, PAIRS0), (1, PAIRS3)):
            for px, py, rule in pairs:
                alpha, side = rule[j]
                cond = (zl == n) & (zh == side) & (x == py) & (y == (py + alpha) % 4)
                give(cond, j, count, 8 * n + 2 * px + q, 4 * n + py)
                count += 1
    send(diag & (q == 0), lambda: copy(norm, nr.at[0], g_s.at[0], g_r.at[0], sib))

    @pl.when(lower)
    def _():
        for s in range(NS):
            own = split(norm[s])
            for j in range(2):
                q_loc[j, s] = mm(split(tiles[2 * s + j]), own, (0, 0))

    @pl.when(diag & (q == 1))
    def _():
        for s in range(NS):
            q_loc[0, s] = mm(split(tiles[2 * s]), split(norm[s]), (0, 0))

    give_q = lower | (diag & (q == 1))
    send(give_q, lambda: copy(q_loc.at[jnp.where(lower, 1 - q, 0)], q_rx, q_s.at[0], q_r.at[0], sib))

    @pl.when(lower | (diag & (q == 0)))
    def _():
        arrived(q_rx, q_r.at[0])

    @pl.when(lower)
    def _():
        for s in range(NS):
            for d in range(4):
                lanes = slice(d * LANES, (d + 1) * LANES)
                q_out[d, s] = q_loc[q, s, :, lanes] + q_rx[s, :, lanes]
        cq_rx[x] = q_out[x]

    for d in range(4):
        send(lower & (x != d), lambda d=d: copy(q_out.at[d], cq_rx.at[x], q_ss.at[d], cq_r.at[x], (8 * zl + 2 * d + q, c)))

    @pl.when(lower)
    def _():
        for j in range(4):
            arrived(nr.at[q, j // 2, pl.ds(j % 2 * HALF, HALF)], n_r.at[j])

    send(lower, lambda: copy(nr.at[q], nr.at[q], g_s.at[1], g_r.at[1], sib))

    def put(s, value):
        for d in range(4):
            p_out[d, s] = value[:, d * LANES : (d + 1) * LANES]

    @pl.when(lower)
    def _():
        arrived(nr.at[1 - q], g_r.at[1])
        for s in range(NS):
            put(s, mm(split(tiles[2 * s]), split(nr[0, s])) + mm(split(tiles[2 * s + 1]), split(nr[1, s])))

    @pl.when(diag & (q == 1))
    def _():
        arrived(nr.at[0], g_r.at[0])
        for s in range(NS):
            put(s, mm(split(tiles[2 * s]), split(nr[0, s])) + mm(split(tiles[2 * s + 1]), split(norm[s])))

    @pl.when(diag & (q == 0))
    def _():
        for s in range(NS):
            put(s, mm(split(tiles[2 * s]), split(norm[s])) + q_rx[s])

    @pl.when(lower | diag)
    def _():
        cp_rx[y] = p_out[y]

    for d in range(4):
        send((lower | diag) & (y != d), lambda d=d: copy(p_out.at[d], cp_rx.at[y], p_ss.at[d], cp_r.at[y], (r, 4 * zh + d)))

    def gather(out, parts, sems, has, here):
        out[...] = jnp.zeros_like(out)
        for m in range(4):

            @pl.when(has(m) & (here != m))
            def _():
                arrived(parts.at[m], sems.at[m])

            @pl.when(has(m))
            def _():
                out[...] += parts[m]

    gather(q_sum, cq_rx, cq_r, lambda m: full | (tri & (y < m)), x)
    mirrored = full | (tri & (y < 3))
    into = jnp.where(full, 1, 0)
    for s in range(NS):
        row, col = 8 * zh + 2 * y + q, 4 * s + x
        mine = (row == r) & (col == c)
        send(
            mirrored & jnp.logical_not(mine),
            lambda s=s, row=row, col=col: copy(q_sum.at[s], qt_rx.at[into], t_s.at[s], t_r.at[into], (row, col)),
        )

        @pl.when(mirrored & mine)
        def _():
            qt_rx[0] = q_sum[s]

    gather(p_sum, cp_rx, cp_r, lambda m: full | (tri & (x >= m)), y)
    far = (c + 4) % NC
    send(work, lambda: copy(p_sum.at[1 - zh], pf_rx, f_s.at[0], f_r.at[0], (r, far)))

    total = p_sum.at[zh]
    first = (zl == 0) & (zh == 0)

    @pl.when(jnp.logical_not(first))
    def _():
        arrived(pf_rx, f_r.at[0])
        total[...] += pf_rx[...]

    @pl.when((x < 3) & jnp.logical_not(tri & (x == y)))
    def _():
        arrived(qt_rx.at[0], t_r.at[0])

    @pl.when(x < 3)
    def _():
        total[...] += qt_rx[0]

    @pl.when(zl == 0)
    def _():
        arrived(qt_rx.at[1], t_r.at[1])
        total[...] += qt_rx[1]

    column = -total[...]
    c_all[c] = column

    part = mm(split(norm[cz]), split(column), (0, 0))
    for a in range(NA):
        d_part[a] = part[a * PIECE : (a + 1) * PIECE]
    for d in range(1, NA):
        to = (r + d) % NA
        send(True, lambda d=d, to=to: copy(d_part.at[to], d_rx.at[r], dp_s.at[d], dp_r.at[r], (to, c)))
    send(True, lambda: copy(c_all.at[c], c_all.at[c], ca_s.at[0], ca_r.at[c], (r, far)))
    acc = base[pl.ds(pl.multiple_of(r * PIECE, PIECE), PIECE), :] - d_part[r]
    for d in range(1, NA):
        of = (r + d) % NA
        arrived(d_rx.at[of], dp_r.at[of])
        acc = acc - d_rx[of]
    d_all[r, c] = acc
    for d in range(1, NC):
        to = (c + d) % NC
        send(True, lambda d=d, to=to: copy(d_all.at[r, c], d_all.at[r, c], da_s.at[d], da_r.at[c], (r, to)))

    def along_y(d):
        return 4 * cz + (cy + d) % 4

    def along_x(d):
        return r - r % 8 + (r + 2 * d) % 8

    for d in range(1, 4):
        send(True, lambda d=d: copy(c_all.at[c], c_all.at[c], ca_s.at[d], ca_r.at[c], (r, along_y(d))))
    for d in range(1, NC):
        of = (c + d) % NC
        arrived(d_all.at[r, of], da_r.at[of])
    near = (r + 8) % NA
    send(True, lambda: copy(d_all.at[r], d_all.at[r], db_s.at[0], db_r.at[k], (near, c)))
    for d in range(1, 4):
        send(True, lambda d=d: copy(d_all.at[r], d_all.at[r], db_s.at[d], db_r.at[k], (along_x(d), c)))
    send(True, lambda: copy(d_all.at[r], d_all.at[r], dc_s.at[0], dc_r.at[k], sib))
    arrived(c_all.at[far], ca_r.at[far])
    for d in range(1, 4):
        send(True, lambda d=d: copy(c_all.at[far], c_all.at[far], ca_s.at[3 + d], ca_r.at[far], (r, along_y(d))))
    arrived(d_all.at[near], db_r.at[near // 2])
    for d in range(1, 4):
        send(True, lambda d=d: copy(d_all.at[near], d_all.at[near], db_s.at[3 + d], db_r.at[near // 2], (along_x(d), c)))
    send(True, lambda: copy(d_all.at[near], d_all.at[near], dc_s.at[1], dc_r.at[near // 2], sib))
    for h in range(2):
        for d in range(1, 4):
            of = (along_x(d) + 8 * h) % NA
            arrived(d_all.at[of], db_r.at[of // 2])
            send(True, lambda d=d, h=h, of=of: copy(d_all.at[of], d_all.at[of], dc_s.at[1 + 3 * h + d], dc_r.at[of // 2], sib))
    for d in range(1, 4):
        for of in (along_y(d), (along_y(d) + 4) % NC):
            arrived(c_all.at[of], ca_r.at[of])
    for m in range(NC):
        arrived(d_all.at[2 * m + 1 - q], dc_r.at[m])
    for cond, make in pending:
        pl.when(cond)(lambda make=make: make().wait_send())


def place(tile_list, tile_valid, c_all, d_all, column_out, diag_out):
    t = pl.program_id(0)
    r = lax.axis_index("row")
    for s in range(NS):
        here = (tile_list[s, r] == 4 * r + t) & (tile_valid[s, r] > 0)
        for j in range(4):
            lanes = slice((4 * s + j) * LANES, (4 * s + j + 1) * LANES)
            column_out[:, lanes] = jnp.where(here, c_all[4 * s + j], 0.0)
            for a in range(4):
                diag_out[s, a * PIECE : (a + 1) * PIECE, j * LANES : (j + 1) * LANES] = d_all[a, 4 * s + j]


def shards(inverse_front, factor, unit_lower, pivot_inverse, tile_list, tile_valid):
    smem = pl.BlockSpec(memory_space=pltpu.SMEM)
    vmem = pl.BlockSpec(memory_space=pltpu.VMEM)
    tiles, norm, base = pl.pallas_call(
        prepare,
        out_shape=(
            jax.ShapeDtypeStruct((4, B, B), F32),
            jax.ShapeDtypeStruct((NS, B, W), F32),
            jax.ShapeDtypeStruct((W, LANES), F32),
        ),
        in_specs=[smem, smem, pl.BlockSpec(memory_space=pl.ANY), vmem, vmem, vmem],
        out_specs=(vmem, vmem, vmem),
        scratch_shapes=[pltpu.SemaphoreType.DMA((4,))],
        name="prepare",
    )(tile_list, tile_valid, inverse_front, factor, unit_lower, pivot_inverse.reshape(NS, 1, W))

    dma = pltpu.SemaphoreType.DMA
    c_all, d_all = pl.pallas_call(
        exchange,
        out_shape=(
            jax.ShapeDtypeStruct((NC, B, LANES), F32),
            jax.ShapeDtypeStruct((NA, NC, PIECE, LANES), F32),
        ),
        in_specs=[vmem, vmem, vmem],
        out_specs=(vmem, vmem),
        scratch_shapes=[
            pltpu.VMEM((2, NS, B, W), F32),
            pltpu.VMEM((2, NS, B, W), F32),
            pltpu.VMEM((NS, B, W), F32),
            pltpu.VMEM((4, NS, B, LANES), F32),
            pltpu.VMEM((4, NS, B, LANES), F32),
            pltpu.VMEM((4, NS, B, LANES), F32),
            pltpu.VMEM((4, NS, B, LANES), F32),
            pltpu.VMEM((NS, B, LANES), F32),
            pltpu.VMEM((NS, B, LANES), F32),
            pltpu.VMEM((B, LANES), F32),
            pltpu.VMEM((2, B, LANES), F32),
            pltpu.VMEM((NA, PIECE, LANES), F32),
            pltpu.VMEM((NA, PIECE, LANES), F32),
            dma((64,)), dma((4,)),
            dma((2,)), dma((2,)),
            dma((1,)), dma((1,)),
            dma((4,)), dma((4,)), dma((4,)), dma((4,)),
            dma((1,)), dma((1,)),
            dma((2,)), dma((2,)),
            dma((NC,)), dma((NC,)),
            dma((NA,)), dma((NA,)),
            dma((NC,)), dma((NC,)),
            dma((NC,)), dma((NC,)),
            dma((NC,)), dma((NC,)),
        ],
        compiler_params=pltpu.CompilerParams(has_side_effects=True),
        name="exchange",
    )(tiles, norm, base)

    whole = lambda shape: pl.BlockSpec(shape, lambda t: (0,) * len(shape))
    return pl.pallas_call(
        place,
        grid=(4,),
        out_shape=(
            jax.ShapeDtypeStruct((4 * B, NS * W), F32),
            jax.ShapeDtypeStruct((NS, W, W), F32),
        ),
        in_specs=[
            smem,
            smem,
            whole((NC, B, LANES)),
            pl.BlockSpec((4, NC, PIECE, LANES), lambda t: (t, 0, 0, 0)),
        ],
        out_specs=(
            pl.BlockSpec((B, NS * W), lambda t: (t, 0)),
            pl.BlockSpec((NS, W // 4, W), lambda t: (0, t, 0)),
        ),
        name="place",
    )(tile_list, tile_valid, c_all, d_all)


def solution(mesh):
    in_specs = (P("row", "col"), P("row", None), P(), P(), P(), P())
    out_specs = (P("row", None), P())
    return jax.shard_map(shards, mesh=mesh, in_specs=in_specs, out_specs=out_specs, check_vma=False)
```

```python
import jax
import jax.numpy as jnp
from jax import lax
from jax.experimental import pallas as pl
from jax.experimental.pallas import tpu as pltpu
from jax.sharding import PartitionSpec as P

B = 256
W = 512
NS = 2
NA = 16
NC = 8
LANES = 128
PIECE = W // NA
MESH = pl.DeviceIdType.MESH
F32 = jnp.float32
BF16 = jnp.bfloat16


def split(x):
    hi = x.astype(BF16)
    return hi, (x - hi.astype(F32)).astype(BF16)


def mm(a, b, dims=(1, 0)):
    def dot(x, y):
        return lax.dot_general(x, y, (((dims[0],), (dims[1],)), ((), ())), preferred_element_type=F32)

    return dot(a[0], b[0]) + (dot(a[0], b[1]) + dot(a[1], b[0]))


FULL = (
    ((0, 1), (0, 1), (0, 0), (0, 0)),
    ((0, 1), (1, 1), (0, 0), (0, 0)),
    ((1, 0), (3, 1), (2, 0), (0, 1)),
    ((2, 1), (0, 0), (1, 1), (1, 0)),
)
PAIRS0 = (
    (1, 0, ((1, 0), (3, 0), (2, 0), (2, 1))),
    (2, 0, ((2, 0), (1, 1), (3, 0), (0, 1))),
    (3, 0, ((0, 0), (1, 0), (3, 0), (3, 1))),
    (2, 1, ((2, 0), (3, 0), (2, 1), (1, 0))),
    (3, 1, ((2, 0), (1, 1), (3, 1), (3, 0))),
    (3, 2, ((3, 1), (1, 0), (3, 0), (3, 0))),
)
PAIRS3 = (
    (1, 0, ((1, 1), (0, 1), (3, 1), (2, 1))),
    (2, 0, ((2, 1), (1, 0), (1, 1), (0, 1))),
    (3, 0, ((3, 1), (0, 0), (1, 1), (3, 0))),
    (2, 1, ((0, 1), (3, 0), (2, 0), (2, 1))),
    (3, 1, ((1, 1), (2, 1), (3, 1), (1, 0))),
    (3, 2, ((0, 1), (2, 0), (3, 1), (1, 1))),
)
HALF = B // 2


def exchange(
    tile_list, tile_valid, front_hbm, factor_hbm, lower_hbm, pivot_hbm, c_all, d_all,
    front, factor, lower_v, pivot, tiles, norm, base, in_s, nr, q_loc, q_rx, p_out, q_out, cp_rx, cq_rx, p_sum, q_sum, pf_rx, qt_rx, d_part, d_rx,
    n_s, n_r, g_s, g_r, q_s, q_r, p_ss, q_ss, cp_r, cq_r, f_s, f_r, t_s, t_r,
    ca_s, ca_r, dp_s, dp_r, da_s, da_r, db_s, db_r, dc_s, dc_r,
):
    r = lax.axis_index("row")
    c = lax.axis_index("col")
    k = r // 2
    q = r % 2
    x = k % 4
    zl = k // 4
    y = cy = c % 4
    zh = cz = c // 4
    sib = (r + 1 - 2 * q, c)
    lower = k > c
    diag = k == c
    full = (zl == 1) & (zh == 0)
    tri = zl == zh
    work = full | tri
    pending = []

    def copy(src, dst, ssem, rsem, dev):
        return pltpu.make_async_remote_copy(
            src_ref=src, dst_ref=dst, send_sem=ssem, recv_sem=rsem, device_id=dev, device_id_type=MESH
        )

    def send(cond, make):
        pl.when(cond)(lambda: make().start())
        pending.append((cond, make))

    def arrived(buf, sem):
        copy(buf, buf, sem, sem, sib).wait_recv()

    fetch = [
        pltpu.make_async_copy(factor_hbm, factor, in_s.at[0]),
        pltpu.make_async_copy(lower_hbm, lower_v, in_s.at[1]),
        pltpu.make_async_copy(pivot_hbm, pivot, in_s.at[2]),
    ]
    for item in fetch:
        item.start()

    @pl.when(lower | diag)
    def _():
        for i in range(4):
            for j in range(8):
                part = front_hbm.at[i * B : (i + 1) * B, j * B : (j + 1) * B]
                pltpu.make_async_copy(part, front.at[i, j], in_s.at[3]).start()

    entry = pltpu.get_barrier_semaphore()

    def greet(cond, dev):
        pl.when(cond)(lambda: pl.semaphore_signal(entry, inc=1, device_id=dev, device_id_type=MESH))

    for d in range(1, NC):
        greet(True, (r, (c + d) % NC))
    for d in range(1, NA):
        greet(True, ((r + d) % NA, c))
    for m in range(NC):
        greet(jnp.logical_not(diag & (c == m)), (2 * c + q, m))
        greet(jnp.logical_not(diag & (k == m)), (2 * m + q, k))

    i0 = lax.broadcasted_iota(jnp.int32, (W, W), 0)
    i1 = lax.broadcasted_iota(jnp.int32, (W, W), 1)
    fetch[0].wait()
    fetch[1].wait()
    for s in range(NS):
        inv = jnp.where(i0 > i1, lower_v[s], jnp.where(i0 == i1, 1.0, 0.0))
        keep = (tile_valid[s, r] > 0).astype(F32)
        norm[s] = mm(split(factor[:, s * W : (s + 1) * W] * keep), split(inv))
    pl.semaphore_wait(entry, jnp.where(diag, 36, 38))

    def give(cond, j, sem, row, col):
        part = pl.ds(j % 2 * HALF, HALF)
        send(cond, lambda: copy(norm.at[j // 2, part], nr.at[q, j // 2, part], n_s.at[sem], n_r.at[j], (row, col)))

    count = 0
    for j in range(4):
        for d in range(4):
            alpha, side = FULL[d][j]
            give((zl == 0) & (zh == side) & ((y - x + 4) % 4 == alpha), j, count, 8 + 2 * ((x + d) % 4) + q, x)
            count += 1
        for n, pairs in ((0, PAIRS0), (1, PAIRS3)):
            for px, py, rule in pairs:
                alpha, side = rule[j]
                cond = (zl == n) & (zh == side) & (x == py) & (y == (py + alpha) % 4)
                give(cond, j, count, 8 * n + 2 * px + q, 4 * n + py)
                count += 1
    send(diag & (q == 0), lambda: copy(norm, nr.at[0], g_s.at[0], g_r.at[0], sib))

    @pl.when(lower | diag)
    def _():
        pltpu.make_async_copy(front, front, in_s.at[3]).wait()
        b0 = lax.broadcasted_iota(jnp.int32, (B, B), 0)
        b1 = lax.broadcasted_iota(jnp.int32, (B, B), 1)
        for s in range(NS):
            for j in range(2):
                tiles[2 * s + j] = front[lax.rem(tile_list[s, r], 4), lax.rem(tile_list[s, 2 * c + j], 8)]

                @pl.when(r == 2 * c + j)
                def _():
                    tile = tiles[2 * s + j]
                    tiles[2 * s + j] = jnp.where(b0 >= b1, tile, tile.T)

    @pl.when(lower)
    def _():
        for s in range(NS):
            own = split(norm[s])
            for j in range(2):
                q_loc[j, s] = mm(split(tiles[2 * s + j]), own, (0, 0))

    @pl.when(diag & (q == 1))
    def _():
        for s in range(NS):
            q_loc[0, s] = mm(split(tiles[2 * s]), split(norm[s]), (0, 0))

    give_q = lower | (diag & (q == 1))
    send(give_q, lambda: copy(q_loc.at[jnp.where(lower, 1 - q, 0)], q_rx, q_s.at[0], q_r.at[0], sib))

    @pl.when(lower | (diag & (q == 0)))
    def _():
        arrived(q_rx, q_r.at[0])

    @pl.when(lower)
    def _():
        for s in range(NS):
            for d in range(4):
                lanes = slice(d * LANES, (d + 1) * LANES)
                q_out[d, s] = q_loc[q, s, :, lanes] + q_rx[s, :, lanes]
        cq_rx[x] = q_out[x]

    for d in range(4):
        send(lower & (x != d), lambda d=d: copy(q_out.at[d], cq_rx.at[x], q_ss.at[d], cq_r.at[x], (8 * zl + 2 * d + q, c)))

    fetch[2].wait()
    for s in range(NS):

        @pl.when(zh == s)
        def _():
            i2 = lax.broadcasted_iota(jnp.int32, (W, LANES), 0)
            i3 = lax.broadcasted_iota(jnp.int32, (W, LANES), 1) + cy * LANES
            lanes = pl.ds(pl.multiple_of(cy * LANES, LANES), LANES)
            inv = jnp.where(i0 > i1, lower_v[s], jnp.where(i0 == i1, 1.0, 0.0))
            part = jnp.where(i2 > i3, lower_v[s, :, lanes], jnp.where(i2 == i3, 1.0, 0.0))
            base[...] = mm(split(inv), split(part * pivot[s : s + 1].T), (0, 0))

    @pl.when(lower)
    def _():
        for j in range(4):
            arrived(nr.at[q, j // 2, pl.ds(j % 2 * HALF, HALF)], n_r.at[j])

    send(lower, lambda: copy(nr.at[q], nr.at[q], g_s.at[1], g_r.at[1], sib))

    def put(s, value):
        for d in range(4):
            p_out[d, s] = value[:, d * LANES : (d + 1) * LANES]

    @pl.when(lower)
    def _():
        arrived(nr.at[1 - q], g_r.at[1])
        for s in range(NS):
            put(s, mm(split(tiles[2 * s]), split(nr[0, s])) + mm(split(tiles[2 * s + 1]), split(nr[1, s])))

    @pl.when(diag & (q == 1))
    def _():
        arrived(nr.at[0], g_r.at[0])
        for s in range(NS):
            put(s, mm(split(tiles[2 * s]), split(nr[0, s])) + mm(split(tiles[2 * s + 1]), split(norm[s])))

    @pl.when(diag & (q == 0))
    def _():
        for s in range(NS):
            put(s, mm(split(tiles[2 * s]), split(norm[s])) + q_rx[s])

    @pl.when(lower | diag)
    def _():
        cp_rx[y] = p_out[y]

    for d in range(4):
        send((lower | diag) & (y != d), lambda d=d: copy(p_out.at[d], cp_rx.at[y], p_ss.at[d], cp_r.at[y], (r, 4 * zh + d)))

    def gather(out, parts, sems, has, here):
        out[...] = jnp.zeros_like(out)
        for m in range(4):

            @pl.when(has(m) & (here != m))
            def _():
                arrived(parts.at[m], sems.at[m])

            @pl.when(has(m))
            def _():
                out[...] += parts[m]

    gather(q_sum, cq_rx, cq_r, lambda m: full | (tri & (y < m)), x)
    mirrored = full | (tri & (y < 3))
    into = jnp.where(full, 1, 0)
    for s in range(NS):
        row, col = 8 * zh + 2 * y + q, 4 * s + x
        mine = (row == r) & (col == c)
        send(
            mirrored & jnp.logical_not(mine),
            lambda s=s, row=row, col=col: copy(q_sum.at[s], qt_rx.at[into], t_s.at[s], t_r.at[into], (row, col)),
        )

        @pl.when(mirrored & mine)
        def _():
            qt_rx[0] = q_sum[s]

    gather(p_sum, cp_rx, cp_r, lambda m: full | (tri & (x >= m)), y)
    far = (c + 4) % NC
    send(work, lambda: copy(p_sum.at[1 - zh], pf_rx, f_s.at[0], f_r.at[0], (r, far)))

    total = p_sum.at[zh]
    first = (zl == 0) & (zh == 0)

    @pl.when(jnp.logical_not(first))
    def _():
        arrived(pf_rx, f_r.at[0])
        total[...] += pf_rx[...]

    @pl.when((x < 3) & jnp.logical_not(tri & (x == y)))
    def _():
        arrived(qt_rx.at[0], t_r.at[0])

    @pl.when(x < 3)
    def _():
        total[...] += qt_rx[0]

    @pl.when(zl == 0)
    def _():
        arrived(qt_rx.at[1], t_r.at[1])
        total[...] += qt_rx[1]

    column = -total[...]
    c_all[c] = column

    part = mm(split(norm[cz]), split(column), (0, 0))
    for a in range(NA):
        d_part[a] = part[a * PIECE : (a + 1) * PIECE]
    for d in range(1, NA):
        to = (r + d) % NA
        send(True, lambda d=d, to=to: copy(d_part.at[to], d_rx.at[r], dp_s.at[d], dp_r.at[r], (to, c)))
    send(True, lambda: copy(c_all.at[c], c_all.at[c], ca_s.at[0], ca_r.at[c], (r, far)))
    acc = base[pl.ds(pl.multiple_of(r * PIECE, PIECE), PIECE), :] - d_part[r]
    for d in range(1, NA):
        of = (r + d) % NA
        arrived(d_rx.at[of], dp_r.at[of])
        acc = acc - d_rx[of]
    d_all[r, c] = acc
    for d in range(1, NC):
        to = (c + d) % NC
        send(True, lambda d=d, to=to: copy(d_all.at[r, c], d_all.at[r, c], da_s.at[d], da_r.at[c], (r, to)))

    def along_y(d):
        return 4 * cz + (cy + d) % 4

    def along_x(d):
        return r - r % 8 + (r + 2 * d) % 8

    for d in range(1, 4):
        send(True, lambda d=d: copy(c_all.at[c], c_all.at[c], ca_s.at[d], ca_r.at[c], (r, along_y(d))))
    for d in range(1, NC):
        of = (c + d) % NC
        arrived(d_all.at[r, of], da_r.at[of])
    near = (r + 8) % NA
    send(True, lambda: copy(d_all.at[r], d_all.at[r], db_s.at[0], db_r.at[k], (near, c)))
    for d in range(1, 4):
        send(True, lambda d=d: copy(d_all.at[r], d_all.at[r], db_s.at[d], db_r.at[k], (along_x(d), c)))
    send(True, lambda: copy(d_all.at[r], d_all.at[r], dc_s.at[0], dc_r.at[k], sib))
    arrived(c_all.at[far], ca_r.at[far])
    for d in range(1, 4):
        send(True, lambda d=d: copy(c_all.at[far], c_all.at[far], ca_s.at[3 + d], ca_r.at[far], (r, along_y(d))))
    arrived(d_all.at[near], db_r.at[near // 2])
    for d in range(1, 4):
        send(True, lambda d=d: copy(d_all.at[near], d_all.at[near], db_s.at[3 + d], db_r.at[near // 2], (along_x(d), c)))
    send(True, lambda: copy(d_all.at[near], d_all.at[near], dc_s.at[1], dc_r.at[near // 2], sib))
    for h in range(2):
        for d in range(1, 4):
            of = (along_x(d) + 8 * h) % NA
            arrived(d_all.at[of], db_r.at[of // 2])
            send(True, lambda d=d, h=h, of=of: copy(d_all.at[of], d_all.at[of], dc_s.at[1 + 3 * h + d], dc_r.at[of // 2], sib))
    for d in range(1, 4):
        for of in (along_y(d), (along_y(d) + 4) % NC):
            arrived(c_all.at[of], ca_r.at[of])
    for m in range(NC):
        arrived(d_all.at[2 * m + 1 - q], dc_r.at[m])
    for cond, make in pending:
        pl.when(cond)(lambda make=make: make().wait_send())


def place(tile_list, tile_valid, c_all, d_all, column_out, diag_out, zeros, cols, block, out_s, d_s):
    r = lax.axis_index("row")
    zeros[...] = jnp.zeros_like(zeros)

    def out(src, s, t):
        row = pl.ds(pl.multiple_of(t * B, B), B)
        return pltpu.make_async_copy(src, column_out.at[row, s * W : (s + 1) * W], out_s.at[s, t])

    live = [tile_valid[s, r] > 0 for s in range(NS)]
    chosen = [tile_list[s, r] - 4 * r for s in range(NS)]
    for s in range(NS):
        for t in range(4):
            pl.when(jnp.logical_not(live[s] & (chosen[s] == t)))(lambda s=s, t=t: out(zeros, s, t).start())
    for s in range(NS):
        for i in range(4):
            cols[s, :, i * LANES : (i + 1) * LANES] = c_all[4 * s + i]
        for t in range(4):
            pl.when(live[s] & (chosen[s] == t))(lambda s=s, t=t: out(cols.at[s], s, t).start())
    writes = []
    for g in range(4):
        rows = slice(4 * g * PIECE, 4 * (g + 1) * PIECE)
        for a in range(4 * g, 4 * g + 4):
            for i in range(NC):
                lanes = slice(i % 4 * LANES, (i % 4 + 1) * LANES)
                block[i // 4, a * PIECE : (a + 1) * PIECE, lanes] = d_all[a, i]
        writes.append(pltpu.make_async_copy(block.at[:, rows], diag_out.at[:, rows], d_s.at[g]))
        writes[-1].start()
    for write in writes:
        write.wait()
    for s in range(NS):
        for t in range(4):
            out(zeros, s, t).wait()


def shards(inverse_front, factor, unit_lower, pivot_inverse, tile_list, tile_valid):
    smem = pl.BlockSpec(memory_space=pltpu.SMEM)
    vmem = pl.BlockSpec(memory_space=pltpu.VMEM)
    hbm = pl.BlockSpec(memory_space=pl.ANY)
    dma = pltpu.SemaphoreType.DMA
    c_all, d_all = pl.pallas_call(
        exchange,
        out_shape=(
            pltpu.VMEM((NC, B, LANES), F32),
            pltpu.VMEM((NA, NC, PIECE, LANES), F32),
        ),
        in_specs=[smem, smem, hbm, hbm, hbm, hbm],
        out_specs=(vmem, vmem),
        scratch_shapes=[
            pltpu.VMEM((4, 8, B, B), F32),
            pltpu.VMEM((B, NS * W), F32),
            pltpu.VMEM((NS, W, W), F32),
            pltpu.VMEM((NS, W), F32),
            pltpu.VMEM((2 * NS, B, B), F32),
            pltpu.VMEM((NS, B, W), F32),
            pltpu.VMEM((W, LANES), F32),
            dma((4,)),
            pltpu.VMEM((2, NS, B, W), F32),
            pltpu.VMEM((2, NS, B, W), F32),
            pltpu.VMEM((NS, B, W), F32),
            pltpu.VMEM((4, NS, B, LANES), F32),
            pltpu.VMEM((4, NS, B, LANES), F32),
            pltpu.VMEM((4, NS, B, LANES), F32),
            pltpu.VMEM((4, NS, B, LANES), F32),
            pltpu.VMEM((NS, B, LANES), F32),
            pltpu.VMEM((NS, B, LANES), F32),
            pltpu.VMEM((B, LANES), F32),
            pltpu.VMEM((2, B, LANES), F32),
            pltpu.VMEM((NA, PIECE, LANES), F32),
            pltpu.VMEM((NA, PIECE, LANES), F32),
            dma((64,)), dma((4,)),
            dma((2,)), dma((2,)),
            dma((1,)), dma((1,)),
            dma((4,)), dma((4,)), dma((4,)), dma((4,)),
            dma((1,)), dma((1,)),
            dma((2,)), dma((2,)),
            dma((NC,)), dma((NC,)),
            dma((NA,)), dma((NA,)),
            dma((NC,)), dma((NC,)),
            dma((NC,)), dma((NC,)),
            dma((NC,)), dma((NC,)),
        ],
        compiler_params=pltpu.CompilerParams(has_side_effects=True, collective_id=0),
        name="exchange",
    )(tile_list, tile_valid, inverse_front, factor, unit_lower, pivot_inverse)

    return pl.pallas_call(
        place,
        out_shape=(
            jax.ShapeDtypeStruct((4 * B, NS * W), F32),
            jax.ShapeDtypeStruct((NS, W, W), F32),
        ),
        in_specs=[smem, smem, vmem, vmem],
        out_specs=(hbm, hbm),
        scratch_shapes=[
            pltpu.VMEM((B, W), F32),
            pltpu.VMEM((NS, B, W), F32),
            pltpu.VMEM((NS, W, W), F32),
            dma((NS, 4)),
            dma((4,)),
        ],
        name="place",
    )(
        tile_list,
        tile_valid,
        pltpu.with_memory_space_constraint(c_all, pltpu.VMEM),
        pltpu.with_memory_space_constraint(d_all, pltpu.VMEM),
    )


def solution(mesh):
    in_specs = (P("row", "col"), P("row", None), P(), P(), P(), P())
    out_specs = (P("row", None), P())
    return jax.shard_map(shards, mesh=mesh, in_specs=in_specs, out_specs=out_specs, check_vma=False)
```

```python
import jax
import jax.numpy as jnp
from jax import lax
from jax.experimental import pallas as pl
from jax.experimental.pallas import tpu as pltpu
from jax.sharding import PartitionSpec as P

B = 256
W = 512
NS = 2
NA = 16
NC = 8
LANES = 128
PIECE = W // NA
MESH = pl.DeviceIdType.MESH
F32 = jnp.float32
BF16 = jnp.bfloat16


def split(x):
    hi = x.astype(BF16)
    return hi, (x - hi.astype(F32)).astype(BF16)


def mm(a, b, dims=(1, 0)):
    def dot(x, y):
        return lax.dot_general(x, y, (((dims[0],), (dims[1],)), ((), ())), preferred_element_type=F32)

    return dot(a[0], b[0]) + (dot(a[0], b[1]) + dot(a[1], b[0]))


FULL = (
    ((0, 0), (0, 1), (0, 1), (0, 0)),
    ((0, 0), (2, 1), (1, 1), (1, 0)),
    ((2, 1), (1, 1), (2, 0), (1, 0)),
    ((3, 0), (2, 0), (2, 1), (3, 1)),
)
PAIRS0 = (
    (1, 0, ((3, 0), (3, 1))),
    (2, 0, ((0, 1), (0, 0))),
    (3, 0, ((0, 1), (0, 0))),
    (2, 1, ((0, 1), (2, 0))),
    (3, 1, ((0, 1), (0, 0))),
    (3, 2, ((3, 0), (0, 1))),
)
PAIRS3 = (
    (1, 0, ((1, 1), (0, 1))),
    (2, 0, ((3, 1), (0, 0))),
    (3, 0, ((0, 1), (3, 1))),
    (2, 1, ((3, 1), (0, 1))),
    (3, 1, ((1, 1), (0, 1))),
    (3, 2, ((1, 1), (0, 1))),
)
HALF = B // 2


def exchange(
    tile_list, tile_valid, front_hbm, factor_hbm, lower_hbm, pivot_hbm, c_all, d_all,
    front, factor, lower_v, pivot, tiles, norm, base, in_s, nr, q_loc, q_rx, p_out, q_out, cp_rx, cq_rx, p_sum, q_sum, pf_rx, qt_rx, d_part, d_rx,
    n_s, n_r, g_s, g_r, q_s, q_r, p_ss, q_ss, cp_r, cq_r, f_s, f_r, t_s, t_r,
    ca_s, ca_r, dp_s, dp_r, da_s, da_r, db_s, db_r, dh_s, dh_r, dc_s, dc_r,
):
    r = lax.axis_index("row")
    c = lax.axis_index("col")
    k = r // 2
    q = r % 2
    x = k % 4
    zl = k // 4
    y = cy = c % 4
    zh = cz = c // 4
    sib = (r + 1 - 2 * q, c)
    lower = k > c
    diag = k == c
    full = (zl == 1) & (zh == 0)
    tri = zl == zh
    work = full | tri
    pending = []

    def copy(src, dst, ssem, rsem, dev):
        return pltpu.make_async_remote_copy(
            src_ref=src, dst_ref=dst, send_sem=ssem, recv_sem=rsem, device_id=dev, device_id_type=MESH
        )

    def send(cond, make):
        pl.when(cond)(lambda: make().start())
        pending.append((cond, make))

    def arrived(buf, sem):
        copy(buf, buf, sem, sem, sib).wait_recv()

    fetch = [
        pltpu.make_async_copy(factor_hbm, factor, in_s.at[0]),
        pltpu.make_async_copy(lower_hbm, lower_v, in_s.at[1]),
        pltpu.make_async_copy(pivot_hbm, pivot, in_s.at[2]),
    ]
    for item in fetch:
        item.start()

    @pl.when(lower | diag)
    def _():
        for i in range(4):
            for j in range(8):
                part = front_hbm.at[i * B : (i + 1) * B, j * B : (j + 1) * B]
                pltpu.make_async_copy(part, front.at[i, j], in_s.at[3]).start()

    entry = pltpu.get_barrier_semaphore()

    def greet(cond, dev):
        pl.when(cond)(lambda: pl.semaphore_signal(entry, inc=1, device_id=dev, device_id_type=MESH))

    for d in range(1, NC):
        greet(True, (r, (c + d) % NC))
    for d in range(1, NA):
        greet(True, ((r + d) % NA, c))
    for m in range(NC):
        greet(jnp.logical_not(diag & (c == m)), (2 * c + q, m))
        greet(jnp.logical_not(diag & (k == m)), (2 * m + q, k))

    i0 = lax.broadcasted_iota(jnp.int32, (W, W), 0)
    i1 = lax.broadcasted_iota(jnp.int32, (W, W), 1)
    fetch[0].wait()
    fetch[1].wait()
    for s in range(NS):
        inv = jnp.where(i0 > i1, lower_v[s], jnp.where(i0 == i1, 1.0, 0.0))
        keep = (tile_valid[s, r] > 0).astype(F32)
        norm[s] = mm(split(factor[:, s * W : (s + 1) * W] * keep), split(inv))
    pl.semaphore_wait(entry, jnp.where(diag, 36, 38))

    def give(cond, s, part, sem, arrival, row, col):
        send(cond, lambda: copy(norm.at[s, part], nr.at[q, s, part], n_s.at[sem], n_r.at[arrival], (row, col)))

    count = 0
    for s in range(NS):
        for j in (2 * s, 2 * s + 1):
            for d in range(4):
                alpha, side = FULL[d][j]
                cond = (zl == 0) & (zh == side) & ((y - x + 4) % 4 == alpha)
                give(cond, s, pl.ds(j % 2 * HALF, HALF), count, j, 8 + 2 * ((x + d) % 4) + q, x)
                count += 1
        for n, pairs in ((0, PAIRS0), (1, PAIRS3)):
            for px, py, rule in pairs:
                alpha, side = rule[s]
                cond = (zl == n) & (zh == side) & (x == py) & (y == (py + alpha) % 4)
                give(cond, s, pl.ds(0, B), count, 2 * s, 8 * n + 2 * px + q, 4 * n + py)
                count += 1
    send(diag & (q == 0), lambda: copy(norm, nr.at[0], g_s.at[0], g_r.at[0], sib))

    @pl.when(lower | diag)
    def _():
        pltpu.make_async_copy(front, front, in_s.at[3]).wait()
        b0 = lax.broadcasted_iota(jnp.int32, (B, B), 0)
        b1 = lax.broadcasted_iota(jnp.int32, (B, B), 1)
        for s in range(NS):
            for j in range(2):
                tiles[2 * s + j] = front[lax.rem(tile_list[s, r], 4), lax.rem(tile_list[s, 2 * c + j], 8)]

                @pl.when(r == 2 * c + j)
                def _():
                    tile = tiles[2 * s + j]
                    tiles[2 * s + j] = jnp.where(b0 >= b1, tile, tile.T)

    @pl.when(lower)
    def _():
        for s in range(NS):
            own = split(norm[s])
            for j in range(2):
                q_loc[j, s] = mm(split(tiles[2 * s + j]), own, (0, 0))

    @pl.when(diag & (q == 1))
    def _():
        for s in range(NS):
            q_loc[0, s] = mm(split(tiles[2 * s]), split(norm[s]), (0, 0))

    give_q = lower | (diag & (q == 1))
    send(give_q, lambda: copy(q_loc.at[jnp.where(lower, 1 - q, 0)], q_rx, q_s.at[0], q_r.at[0], sib))

    @pl.when(lower | (diag & (q == 0)))
    def _():
        arrived(q_rx, q_r.at[0])

    @pl.when(lower)
    def _():
        for s in range(NS):
            for d in range(4):
                lanes = slice(d * LANES, (d + 1) * LANES)
                q_out[d, s] = q_loc[q, s, :, lanes] + q_rx[s, :, lanes]
        cq_rx[x] = q_out[x]

    for d in range(4):
        send(lower & (x != d), lambda d=d: copy(q_out.at[d], cq_rx.at[x], q_ss.at[d], cq_r.at[x], (8 * zl + 2 * d + q, c)))

    fetch[2].wait()
    for s in range(NS):

        @pl.when(zh == s)
        def _():
            i2 = lax.broadcasted_iota(jnp.int32, (W, LANES), 0)
            i3 = lax.broadcasted_iota(jnp.int32, (W, LANES), 1) + cy * LANES
            lanes = pl.ds(pl.multiple_of(cy * LANES, LANES), LANES)
            inv = jnp.where(i0 > i1, lower_v[s], jnp.where(i0 == i1, 1.0, 0.0))
            part = jnp.where(i2 > i3, lower_v[s, :, lanes], jnp.where(i2 == i3, 1.0, 0.0))
            base[...] = mm(split(inv), split(part * pivot[s : s + 1].T), (0, 0))

    for s in range(NS):

        @pl.when(full)
        def _():
            for j in (2 * s, 2 * s + 1):
                arrived(nr.at[q, s, pl.ds(j % 2 * HALF, HALF)], n_r.at[j])

        @pl.when(lower & tri)
        def _():
            arrived(nr.at[q, s], n_r.at[2 * s])

        send(lower, lambda s=s: copy(nr.at[q, s], nr.at[q, s], g_s.at[1 + s], g_r.at[1 + s], sib))

        def put(value):
            for d in range(4):
                p_out[s, d] = value[:, d * LANES : (d + 1) * LANES]
            cp_rx[s, y] = p_out[s, y]

        @pl.when(lower)
        def _():
            arrived(nr.at[1 - q, s], g_r.at[1 + s])
            put(mm(split(tiles[2 * s]), split(nr[0, s])) + mm(split(tiles[2 * s + 1]), split(nr[1, s])))

        @pl.when(diag & (q == 1))
        def _():
            if s == 0:
                arrived(nr.at[0], g_r.at[0])
            put(mm(split(tiles[2 * s]), split(nr[0, s])) + mm(split(tiles[2 * s + 1]), split(norm[s])))

        @pl.when(diag & (q == 0))
        def _():
            put(mm(split(tiles[2 * s]), split(norm[s])) + q_rx[s])

        for d in range(4):
            send(
                (lower | diag) & (y != d),
                lambda s=s, d=d: copy(p_out.at[s, d], cp_rx.at[s, y], p_ss.at[s, d], cp_r.at[s, y], (r, 4 * zh + d)),
            )

    def gather(out, parts, sems, has, here):
        out[...] = jnp.zeros_like(out)
        for m in range(4):

            @pl.when(has(m) & (here != m))
            def _():
                arrived(parts.at[m], sems.at[m])

            @pl.when(has(m))
            def _():
                out[...] += parts[m]

    gather(q_sum, cq_rx, cq_r, lambda m: full | (tri & (y < m)), x)
    mirrored = full | (tri & (y < 3))
    into = jnp.where(full, 1, 0)
    for s in range(NS):
        row, col = 8 * zh + 2 * y + q, 4 * s + x
        mine = (row == r) & (col == c)
        send(
            mirrored & jnp.logical_not(mine),
            lambda s=s, row=row, col=col: copy(q_sum.at[s], qt_rx.at[into], t_s.at[s], t_r.at[into], (row, col)),
        )

        @pl.when(mirrored & mine)
        def _():
            qt_rx[0] = q_sum[s]

    far = (c + 4) % NC
    for s in range(NS):
        gather(p_sum.at[s], cp_rx.at[s], cp_r.at[s], lambda m: full | (tri & (x >= m)), y)
        send(work & (zh == 1 - s), lambda s=s: copy(p_sum.at[s], pf_rx, f_s.at[0], f_r.at[0], (r, far)))

    total = p_sum.at[zh]
    first = (zl == 0) & (zh == 0)

    @pl.when(jnp.logical_not(first))
    def _():
        arrived(pf_rx, f_r.at[0])
        total[...] += pf_rx[...]

    @pl.when((x < 3) & jnp.logical_not(tri & (x == y)))
    def _():
        arrived(qt_rx.at[0], t_r.at[0])

    @pl.when(x < 3)
    def _():
        total[...] += qt_rx[0]

    @pl.when(zl == 0)
    def _():
        arrived(qt_rx.at[1], t_r.at[1])
        total[...] += qt_rx[1]

    column = -total[...]
    c_all[c] = column

    part = mm(split(norm[cz]), split(column), (0, 0))
    for a in range(NA):
        d_part[a] = part[a * PIECE : (a + 1) * PIECE]
    for d in range(1, NA):
        to = (r + d) % NA
        send(True, lambda d=d, to=to: copy(d_part.at[to], d_rx.at[r], dp_s.at[d], dp_r.at[r], (to, c)))
    def along_y(d):
        return 4 * cz + (cy + d) % 4

    def along_x(d):
        return r - r % 8 + (r + 2 * d) % 8

    for d in range(1, 4):
        send(True, lambda d=d: copy(c_all.at[c], c_all.at[c], ca_s.at[d], ca_r.at[c], (r, along_y(d))))
    acc = base[pl.ds(pl.multiple_of(r * PIECE, PIECE), PIECE), :] - d_part[r]
    for d in range(1, NA):
        of = (r + d) % NA
        arrived(d_rx.at[of], dp_r.at[of])
        acc = acc - d_rx[of]
    d_all[r, c] = acc
    for d in range(1, NC):
        to = (c + d) % NC
        send(True, lambda d=d, to=to: copy(d_all.at[r, c], d_all.at[r, c], da_s.at[d], da_r.at[c], (r, to)))

    for d in range(1, NC):
        of = (c + d) % NC
        arrived(d_all.at[r, of], da_r.at[of])
    near = (r + 8) % NA
    send(True, lambda: copy(d_all.at[r], d_all.at[r], db_s.at[0], db_r.at[k], (near, c)))
    for d in range(1, 4):
        send(True, lambda d=d: copy(d_all.at[r], d_all.at[r], db_s.at[d], db_r.at[k], (along_x(d), c)))
    send(True, lambda: copy(c_all.at[c], c_all.at[c], ca_s.at[0], ca_r.at[c], (r, far)))
    send(True, lambda: copy(d_all.at[r], d_all.at[r], dc_s.at[0], dc_r.at[k], sib))
    first_half, second_half = pl.ds(0, NC // 2), pl.ds(NC // 2, NC // 2)
    arrived(d_all.at[near], db_r.at[near // 2])
    for d in range(1, 4):
        part = d_all.at[near, first_half]
        send(True, lambda d=d, part=part: copy(part, part, db_s.at[3 + d], dh_r.at[0, near // 2], (along_x(d), c)))
    send(True, lambda: copy(d_all.at[near], d_all.at[near], dc_s.at[1], dc_r.at[near // 2], sib))
    arrived(c_all.at[far], ca_r.at[far])
    for d in range(1, 4):
        send(True, lambda d=d: copy(c_all.at[far], c_all.at[far], ca_s.at[3 + d], ca_r.at[far], (r, along_y(d))))
    for d in range(1, 4):
        of = along_x(d)
        arrived(d_all.at[of], db_r.at[of // 2])
        part = d_all.at[of, second_half]
        send(True, lambda d=d, of=of, part=part: copy(part, part, dh_s.at[d], dh_r.at[1, of // 2], (near, c)))
        send(True, lambda d=d, of=of: copy(d_all.at[of], d_all.at[of], dc_s.at[1 + d], dc_r.at[of // 2], sib))
    for d in range(1, 4):
        of = (along_x(d) + 8) % NA
        arrived(d_all.at[of, first_half], dh_r.at[0, of // 2])
        arrived(d_all.at[of, second_half], dh_r.at[1, of // 2])
        send(True, lambda d=d, of=of: copy(d_all.at[of], d_all.at[of], dc_s.at[4 + d], dc_r.at[of // 2], sib))
    for d in range(1, 4):
        for of in (along_y(d), (along_y(d) + 4) % NC):
            arrived(c_all.at[of], ca_r.at[of])
    for m in range(NC):
        arrived(d_all.at[2 * m + 1 - q], dc_r.at[m])
    for cond, make in pending:
        pl.when(cond)(lambda make=make: make().wait_send())


def place(tile_list, tile_valid, c_all, d_all, column_out, diag_out, zeros, cols, block, out_s, d_s):
    r = lax.axis_index("row")
    zeros[...] = jnp.zeros_like(zeros)

    def out(src, s, t):
        row = pl.ds(pl.multiple_of(t * B, B), B)
        return pltpu.make_async_copy(src, column_out.at[row, s * W : (s + 1) * W], out_s.at[s, t])

    live = [tile_valid[s, r] > 0 for s in range(NS)]
    chosen = [tile_list[s, r] - 4 * r for s in range(NS)]
    for s in range(NS):
        for t in range(4):
            pl.when(jnp.logical_not(live[s] & (chosen[s] == t)))(lambda s=s, t=t: out(zeros, s, t).start())
    for s in range(NS):
        for i in range(4):
            cols[s, :, i * LANES : (i + 1) * LANES] = c_all[4 * s + i]
        for t in range(4):
            pl.when(live[s] & (chosen[s] == t))(lambda s=s, t=t: out(cols.at[s], s, t).start())
    writes = []
    for g in range(4):
        rows = slice(4 * g * PIECE, 4 * (g + 1) * PIECE)
        for a in range(4 * g, 4 * g + 4):
            for i in range(NC):
                lanes = slice(i % 4 * LANES, (i % 4 + 1) * LANES)
                block[i // 4, a * PIECE : (a + 1) * PIECE, lanes] = d_all[a, i]
        writes.append(pltpu.make_async_copy(block.at[:, rows], diag_out.at[:, rows], d_s.at[g]))
        writes[-1].start()
    for write in writes:
        write.wait()
    for s in range(NS):
        for t in range(4):
            out(zeros, s, t).wait()


def shards(inverse_front, factor, unit_lower, pivot_inverse, tile_list, tile_valid):
    smem = pl.BlockSpec(memory_space=pltpu.SMEM)
    vmem = pl.BlockSpec(memory_space=pltpu.VMEM)
    hbm = pl.BlockSpec(memory_space=pl.ANY)
    dma = pltpu.SemaphoreType.DMA
    c_all, d_all = pl.pallas_call(
        exchange,
        out_shape=(
            pltpu.VMEM((NC, B, LANES), F32),
            pltpu.VMEM((NA, NC, PIECE, LANES), F32),
        ),
        in_specs=[smem, smem, hbm, hbm, hbm, hbm],
        out_specs=(vmem, vmem),
        scratch_shapes=[
            pltpu.VMEM((4, 8, B, B), F32),
            pltpu.VMEM((B, NS * W), F32),
            pltpu.VMEM((NS, W, W), F32),
            pltpu.VMEM((NS, W), F32),
            pltpu.VMEM((2 * NS, B, B), F32),
            pltpu.VMEM((NS, B, W), F32),
            pltpu.VMEM((W, LANES), F32),
            dma((4,)),
            pltpu.VMEM((2, NS, B, W), F32),
            pltpu.VMEM((2, NS, B, W), F32),
            pltpu.VMEM((NS, B, W), F32),
            pltpu.VMEM((NS, 4, B, LANES), F32),
            pltpu.VMEM((4, NS, B, LANES), F32),
            pltpu.VMEM((NS, 4, B, LANES), F32),
            pltpu.VMEM((4, NS, B, LANES), F32),
            pltpu.VMEM((NS, B, LANES), F32),
            pltpu.VMEM((NS, B, LANES), F32),
            pltpu.VMEM((B, LANES), F32),
            pltpu.VMEM((2, B, LANES), F32),
            pltpu.VMEM((NA, PIECE, LANES), F32),
            pltpu.VMEM((NA, PIECE, LANES), F32),
            dma((40,)), dma((4,)),
            dma((3,)), dma((3,)),
            dma((1,)), dma((1,)),
            dma((NS, 4)), dma((4,)), dma((NS, 4)), dma((4,)),
            dma((1,)), dma((1,)),
            dma((2,)), dma((2,)),
            dma((NC,)), dma((NC,)),
            dma((NA,)), dma((NA,)),
            dma((NC,)), dma((NC,)),
            dma((NC,)), dma((NC,)),
            dma((4,)), dma((2, NC)),
            dma((NC,)), dma((NC,)),
        ],
        compiler_params=pltpu.CompilerParams(has_side_effects=True, collective_id=0),
        name="exchange",
    )(tile_list, tile_valid, inverse_front, factor, unit_lower, pivot_inverse)

    return pl.pallas_call(
        place,
        out_shape=(
            jax.ShapeDtypeStruct((4 * B, NS * W), F32),
            jax.ShapeDtypeStruct((NS, W, W), F32),
        ),
        in_specs=[smem, smem, vmem, vmem],
        out_specs=(hbm, hbm),
        scratch_shapes=[
            pltpu.VMEM((B, W), F32),
            pltpu.VMEM((NS, B, W), F32),
            pltpu.VMEM((NS, W, W), F32),
            dma((NS, 4)),
            dma((4,)),
        ],
        name="place",
    )(
        tile_list,
        tile_valid,
        pltpu.with_memory_space_constraint(c_all, pltpu.VMEM),
        pltpu.with_memory_space_constraint(d_all, pltpu.VMEM),
    )


def solution(mesh):
    in_specs = (P("row", "col"), P("row", None), P(), P(), P(), P())
    out_specs = (P("row", None), P())
    return jax.shard_map(shards, mesh=mesh, in_specs=in_specs, out_specs=out_specs, check_vma=False)
```

```python
import jax
import jax.numpy as jnp
from jax import lax
from jax.experimental import pallas as pl
from jax.experimental.pallas import tpu as pltpu
from jax.sharding import PartitionSpec as P

B = 256
W = 512
NS = 2
NA = 16
NC = 8
LANES = 128
PIECE = W // NA
MESH = pl.DeviceIdType.MESH
F32 = jnp.float32
BF16 = jnp.bfloat16


def split(x):
    hi = x.astype(BF16)
    return hi, (x - hi.astype(F32)).astype(BF16)


def mm(a, b, dims=(1, 0)):
    def dot(x, y):
        return lax.dot_general(x, y, (((dims[0],), (dims[1],)), ((), ())), preferred_element_type=F32)

    return dot(a[0], b[0]) + (dot(a[0], b[1]) + dot(a[1], b[0]))


FULL = (
    ((0, 0), (0, 1), (0, 1), (0, 0)),
    ((0, 0), (2, 1), (1, 1), (1, 0)),
    ((2, 1), (1, 1), (2, 0), (1, 0)),
    ((3, 0), (2, 0), (2, 1), (3, 1)),
)
PAIRS0 = (
    (1, 0, ((3, 0), (3, 1))),
    (2, 0, ((0, 1), (0, 0))),
    (3, 0, ((0, 1), (0, 0))),
    (2, 1, ((0, 1), (2, 0))),
    (3, 1, ((0, 1), (0, 0))),
    (3, 2, ((3, 0), (0, 1))),
)
PAIRS3 = (
    (1, 0, ((1, 1), (0, 1))),
    (2, 0, ((3, 1), (0, 0))),
    (3, 0, ((0, 1), (3, 1))),
    (2, 1, ((3, 1), (0, 1))),
    (3, 1, ((1, 1), (0, 1))),
    (3, 2, ((1, 1), (0, 1))),
)
HALF = B // 2


def exchange(
    tile_list, tile_valid, front_hbm, factor_hbm, lower_hbm, pivot_hbm, c_all, d_all,
    front, factor, lower_v, pivot, tiles, norm, base, in_s, nr, q_loc, q_rx, p_out, q_out, cp_rx, cq_rx, p_sum, q_sum, pf_rx, qt_rx, d_part, d_rx,
    n_s, n_r, g_s, g_r, q_s, q_r, p_ss, q_ss, cp_r, cq_r, f_s, f_r, t_s, t_r,
    ca_s, ca_r, dp_s, dp_r, da_s, da_r, db_s, db_r, dh_s, dh_r, dc_s, dc_r,
):
    r = lax.axis_index("row")
    c = lax.axis_index("col")
    k = r // 2
    q = r % 2
    x = k % 4
    zl = k // 4
    y = cy = c % 4
    zh = cz = c // 4
    sib = (r + 1 - 2 * q, c)
    lower = k > c
    diag = k == c
    full = (zl == 1) & (zh == 0)
    tri = zl == zh
    work = full | tri
    pending = []

    def copy(src, dst, ssem, rsem, dev):
        return pltpu.make_async_remote_copy(
            src_ref=src, dst_ref=dst, send_sem=ssem, recv_sem=rsem, device_id=dev, device_id_type=MESH
        )

    def send(cond, make):
        pl.when(cond)(lambda: make().start())
        pending.append((cond, make))

    def arrived(buf, sem):
        copy(buf, buf, sem, sem, sib).wait_recv()

    fetch = [
        pltpu.make_async_copy(factor_hbm, factor, in_s.at[0]),
        pltpu.make_async_copy(lower_hbm.at[0], lower_v.at[0], in_s.at[1]),
        pltpu.make_async_copy(lower_hbm.at[1], lower_v.at[1], in_s.at[2]),
        pltpu.make_async_copy(pivot_hbm, pivot, in_s.at[4]),
    ]
    for item in fetch:
        item.start()

    entry = pltpu.get_barrier_semaphore()

    def greet(cond, dev):
        pl.when(cond)(lambda: pl.semaphore_signal(entry, inc=1, device_id=dev, device_id_type=MESH))

    for d in range(1, NC):
        greet(True, (r, (c + d) % NC))
    for d in range(1, NA):
        greet(True, ((r + d) % NA, c))
    for m in range(NC):
        greet(jnp.logical_not(diag & (c == m)), (2 * c + q, m))
        greet(jnp.logical_not(diag & (k == m)), (2 * m + q, k))

    i0 = lax.broadcasted_iota(jnp.int32, (W, W), 0)
    i1 = lax.broadcasted_iota(jnp.int32, (W, W), 1)
    def normalize(s):
        fetch[1 + s].wait()
        inv = jnp.where(i0 > i1, lower_v[s], jnp.where(i0 == i1, 1.0, 0.0))
        keep = (tile_valid[s, r] > 0).astype(F32)
        norm[s] = mm(split(factor[:, s * W : (s + 1) * W] * keep), split(inv))

    fetch[0].wait()
    normalize(0)
    pl.semaphore_wait(entry, jnp.where(diag, 36, 38))

    def give(cond, s, part, sem, arrival, row, col):
        send(cond, lambda: copy(norm.at[s, part], nr.at[q, s, part], n_s.at[sem], n_r.at[arrival], (row, col)))

    count = 0
    for s in range(NS):
        if s == 1:
            normalize(1)
        for j in (2 * s, 2 * s + 1):
            for d in range(4):
                alpha, side = FULL[d][j]
                cond = (zl == 0) & (zh == side) & ((y - x + 4) % 4 == alpha)
                give(cond, s, pl.ds(j % 2 * HALF, HALF), count, j, 8 + 2 * ((x + d) % 4) + q, x)
                count += 1
        for n, pairs in ((0, PAIRS0), (1, PAIRS3)):
            for px, py, rule in pairs:
                alpha, side = rule[s]
                cond = (zl == n) & (zh == side) & (x == py) & (y == (py + alpha) % 4)
                give(cond, s, pl.ds(0, B), count, 2 * s, 8 * n + 2 * px + q, 4 * n + py)
                count += 1
    send(diag & (q == 0), lambda: copy(norm, nr.at[0], g_s.at[0], g_r.at[0], sib))

    @pl.when(lower | diag)
    def _():
        for i in range(4):
            for j in range(8):
                part = front_hbm.at[i * B : (i + 1) * B, j * B : (j + 1) * B]
                pltpu.make_async_copy(part, front.at[i, j], in_s.at[3]).start()

    @pl.when(lower | diag)
    def _():
        pltpu.make_async_copy(front, front, in_s.at[3]).wait()
        b0 = lax.broadcasted_iota(jnp.int32, (B, B), 0)
        b1 = lax.broadcasted_iota(jnp.int32, (B, B), 1)
        for s in range(NS):
            for j in range(2):
                tiles[2 * s + j] = front[lax.rem(tile_list[s, r], 4), lax.rem(tile_list[s, 2 * c + j], 8)]

                @pl.when(r == 2 * c + j)
                def _():
                    tile = tiles[2 * s + j]
                    tiles[2 * s + j] = jnp.where(b0 >= b1, tile, tile.T)

    @pl.when(lower)
    def _():
        for s in range(NS):
            own = split(norm[s])
            for j in range(2):
                q_loc[j, s] = mm(split(tiles[2 * s + j]), own, (0, 0))

    @pl.when(diag & (q == 1))
    def _():
        for s in range(NS):
            q_loc[0, s] = mm(split(tiles[2 * s]), split(norm[s]), (0, 0))

    give_q = lower | (diag & (q == 1))
    send(give_q, lambda: copy(q_loc.at[jnp.where(lower, 1 - q, 0)], q_rx, q_s.at[0], q_r.at[0], sib))

    @pl.when(lower | (diag & (q == 0)))
    def _():
        arrived(q_rx, q_r.at[0])

    @pl.when(lower)
    def _():
        for s in range(NS):
            for d in range(4):
                lanes = slice(d * LANES, (d + 1) * LANES)
                q_out[d, s] = q_loc[q, s, :, lanes] + q_rx[s, :, lanes]
        cq_rx[x] = q_out[x]

    for i in (2, 1, 3):
        d = (x + i) % 4
        send(lower, lambda i=i, d=d: copy(q_out.at[d], cq_rx.at[x], q_ss.at[i], cq_r.at[x], (8 * zl + 2 * d + q, c)))

    fetch[3].wait()
    for s in range(NS):

        @pl.when(zh == s)
        def _():
            i2 = lax.broadcasted_iota(jnp.int32, (W, LANES), 0)
            i3 = lax.broadcasted_iota(jnp.int32, (W, LANES), 1) + cy * LANES
            lanes = pl.ds(pl.multiple_of(cy * LANES, LANES), LANES)
            inv = jnp.where(i0 > i1, lower_v[s], jnp.where(i0 == i1, 1.0, 0.0))
            part = jnp.where(i2 > i3, lower_v[s, :, lanes], jnp.where(i2 == i3, 1.0, 0.0))
            base[...] = mm(split(inv), split(part * pivot[s : s + 1].T), (0, 0))

    for s in range(NS):

        @pl.when(full)
        def _():
            for j in (2 * s, 2 * s + 1):
                arrived(nr.at[q, s, pl.ds(j % 2 * HALF, HALF)], n_r.at[j])

        @pl.when(lower & tri)
        def _():
            arrived(nr.at[q, s], n_r.at[2 * s])

        send(lower, lambda s=s: copy(nr.at[q, s], nr.at[q, s], g_s.at[1 + s], g_r.at[1 + s], sib))

        def put(value):
            for d in range(4):
                p_out[s, d] = value[:, d * LANES : (d + 1) * LANES]
            cp_rx[s, y] = p_out[s, y]

        @pl.when(lower)
        def _():
            arrived(nr.at[1 - q, s], g_r.at[1 + s])
            put(mm(split(tiles[2 * s]), split(nr[0, s])) + mm(split(tiles[2 * s + 1]), split(nr[1, s])))

        @pl.when(diag & (q == 1))
        def _():
            if s == 0:
                arrived(nr.at[0], g_r.at[0])
            put(mm(split(tiles[2 * s]), split(nr[0, s])) + mm(split(tiles[2 * s + 1]), split(norm[s])))

        @pl.when(diag & (q == 0))
        def _():
            put(mm(split(tiles[2 * s]), split(norm[s])) + q_rx[s])

        for i in (2, 1, 3):
            d = (y + i) % 4
            send(
                lower | diag,
                lambda s=s, i=i, d=d: copy(p_out.at[s, d], cp_rx.at[s, y], p_ss.at[s, i], cp_r.at[s, y], (r, 4 * zh + d)),
            )

    def gather(out, parts, sems, has, here):
        out[...] = jnp.zeros_like(out)
        for m in range(4):

            @pl.when(has(m) & (here != m))
            def _():
                arrived(parts.at[m], sems.at[m])

            @pl.when(has(m))
            def _():
                out[...] += parts[m]

    gather(q_sum, cq_rx, cq_r, lambda m: full | (tri & (y < m)), x)
    mirrored = full | (tri & (y < 3))
    into = jnp.where(full, 1, 0)
    for s in range(NS):
        row, col = 8 * zh + 2 * y + q, 4 * s + x
        mine = (row == r) & (col == c)
        send(
            mirrored & jnp.logical_not(mine),
            lambda s=s, row=row, col=col: copy(q_sum.at[s], qt_rx.at[into], t_s.at[s], t_r.at[into], (row, col)),
        )

        @pl.when(mirrored & mine)
        def _():
            qt_rx[0] = q_sum[s]

    far = (c + 4) % NC
    for s in range(NS):
        gather(p_sum.at[s], cp_rx.at[s], cp_r.at[s], lambda m: full | (tri & (x >= m)), y)
        send(work & (zh == 1 - s), lambda s=s: copy(p_sum.at[s], pf_rx, f_s.at[0], f_r.at[0], (r, far)))

    total = p_sum.at[zh]
    first = (zl == 0) & (zh == 0)

    @pl.when(jnp.logical_not(first))
    def _():
        arrived(pf_rx, f_r.at[0])
        total[...] += pf_rx[...]

    @pl.when((x < 3) & jnp.logical_not(tri & (x == y)))
    def _():
        arrived(qt_rx.at[0], t_r.at[0])

    @pl.when(x < 3)
    def _():
        total[...] += qt_rx[0]

    @pl.when(zl == 0)
    def _():
        arrived(qt_rx.at[1], t_r.at[1])
        total[...] += qt_rx[1]

    column = -total[...]
    c_all[c] = column

    part = mm(split(norm[cz]), split(column), (0, 0))
    for a in range(NA):
        d_part[a] = part[a * PIECE : (a + 1) * PIECE]
    for d in range(1, NA):
        to = (r + d) % NA
        send(True, lambda d=d, to=to: copy(d_part.at[to], d_rx.at[r], dp_s.at[d], dp_r.at[r], (to, c)))
    def along_y(d):
        return 4 * cz + (cy + d) % 4

    def along_x(d):
        return r - r % 8 + (r + 2 * d) % 8

    acc = base[pl.ds(pl.multiple_of(r * PIECE, PIECE), PIECE), :] - d_part[r]
    for d in range(1, NA):
        of = (r + d) % NA
        arrived(d_rx.at[of], dp_r.at[of])
        acc = acc - d_rx[of]
    d_all[r, c] = acc
    for d in range(1, NC):
        to = (c + d) % NC
        send(True, lambda d=d, to=to: copy(d_all.at[r, c], d_all.at[r, c], da_s.at[d], da_r.at[c], (r, to)))

    for d in range(1, NC):
        of = (c + d) % NC
        arrived(d_all.at[r, of], da_r.at[of])
    near = (r + 8) % NA
    send(True, lambda: copy(d_all.at[r], d_all.at[r], db_s.at[0], db_r.at[k], (near, c)))
    for d in (2, 1, 3):
        send(True, lambda d=d: copy(d_all.at[r], d_all.at[r], db_s.at[d], db_r.at[k], (along_x(d), c)))
    for d in (2, 1, 3):
        send(True, lambda d=d: copy(c_all.at[c], c_all.at[c], ca_s.at[d], ca_r.at[c], (r, along_y(d))))
    send(True, lambda: copy(c_all.at[c], c_all.at[c], ca_s.at[0], ca_r.at[c], (r, far)))
    send(True, lambda: copy(d_all.at[r], d_all.at[r], dc_s.at[0], dc_r.at[k], sib))
    first_half, second_half = pl.ds(0, NC // 2), pl.ds(NC // 2, NC // 2)
    arrived(d_all.at[near], db_r.at[near // 2])
    for d in (2, 1, 3):
        part = d_all.at[near, first_half]
        send(True, lambda d=d, part=part: copy(part, part, db_s.at[3 + d], dh_r.at[0, near // 2], (along_x(d), c)))
    send(True, lambda: copy(d_all.at[near], d_all.at[near], dc_s.at[1], dc_r.at[near // 2], sib))
    arrived(c_all.at[far], ca_r.at[far])
    for d in (2, 1, 3):
        send(True, lambda d=d: copy(c_all.at[far], c_all.at[far], ca_s.at[3 + d], ca_r.at[far], (r, along_y(d))))
    for d in range(1, 4):
        of = along_x(d)
        arrived(d_all.at[of], db_r.at[of // 2])
        part = d_all.at[of, second_half]
        send(True, lambda d=d, of=of, part=part: copy(part, part, dh_s.at[d], dh_r.at[1, of // 2], (near, c)))
        send(True, lambda d=d, of=of: copy(d_all.at[of], d_all.at[of], dc_s.at[1 + d], dc_r.at[of // 2], sib))
    for d in range(1, 4):
        of = (along_x(d) + 8) % NA
        arrived(d_all.at[of, first_half], dh_r.at[0, of // 2])
        arrived(d_all.at[of, second_half], dh_r.at[1, of // 2])
        send(True, lambda d=d, of=of: copy(d_all.at[of], d_all.at[of], dc_s.at[4 + d], dc_r.at[of // 2], sib))
    for d in range(1, 4):
        for of in (along_y(d), (along_y(d) + 4) % NC):
            arrived(c_all.at[of], ca_r.at[of])
    for m in range(NC):
        arrived(d_all.at[2 * m + 1 - q], dc_r.at[m])
    for cond, make in pending:
        pl.when(cond)(lambda make=make: make().wait_send())


def place(tile_list, tile_valid, c_all, d_all, column_out, diag_out, zeros, cols, block, out_s, d_s):
    r = lax.axis_index("row")
    zeros[...] = jnp.zeros_like(zeros)

    def out(src, s, t):
        row = pl.ds(pl.multiple_of(t * B, B), B)
        return pltpu.make_async_copy(src, column_out.at[row, s * W : (s + 1) * W], out_s.at[s, t])

    live = [tile_valid[s, r] > 0 for s in range(NS)]
    chosen = [tile_list[s, r] - 4 * r for s in range(NS)]
    for s in range(NS):
        for t in range(4):
            pl.when(jnp.logical_not(live[s] & (chosen[s] == t)))(lambda s=s, t=t: out(zeros, s, t).start())
    for s in range(NS):
        for i in range(4):
            cols[s, :, i * LANES : (i + 1) * LANES] = c_all[4 * s + i]
        for t in range(4):
            pl.when(live[s] & (chosen[s] == t))(lambda s=s, t=t: out(cols.at[s], s, t).start())
    writes = []
    for g in range(4):
        rows = slice(4 * g * PIECE, 4 * (g + 1) * PIECE)
        for a in range(4 * g, 4 * g + 4):
            for i in range(NC):
                lanes = slice(i % 4 * LANES, (i % 4 + 1) * LANES)
                block[i // 4, a * PIECE : (a + 1) * PIECE, lanes] = d_all[a, i]
        writes.append(pltpu.make_async_copy(block.at[:, rows], diag_out.at[:, rows], d_s.at[g]))
        writes[-1].start()
    for write in writes:
        write.wait()
    for s in range(NS):
        for t in range(4):
            out(zeros, s, t).wait()


def shards(inverse_front, factor, unit_lower, pivot_inverse, tile_list, tile_valid):
    smem = pl.BlockSpec(memory_space=pltpu.SMEM)
    vmem = pl.BlockSpec(memory_space=pltpu.VMEM)
    hbm = pl.BlockSpec(memory_space=pl.ANY)
    dma = pltpu.SemaphoreType.DMA
    c_all, d_all = pl.pallas_call(
        exchange,
        out_shape=(
            pltpu.VMEM((NC, B, LANES), F32),
            pltpu.VMEM((NA, NC, PIECE, LANES), F32),
        ),
        in_specs=[smem, smem, hbm, hbm, hbm, hbm],
        out_specs=(vmem, vmem),
        scratch_shapes=[
            pltpu.VMEM((4, 8, B, B), F32),
            pltpu.VMEM((B, NS * W), F32),
            pltpu.VMEM((NS, W, W), F32),
            pltpu.VMEM((NS, W), F32),
            pltpu.VMEM((2 * NS, B, B), F32),
            pltpu.VMEM((NS, B, W), F32),
            pltpu.VMEM((W, LANES), F32),
            dma((5,)),
            pltpu.VMEM((2, NS, B, W), F32),
            pltpu.VMEM((2, NS, B, W), F32),
            pltpu.VMEM((NS, B, W), F32),
            pltpu.VMEM((NS, 4, B, LANES), F32),
            pltpu.VMEM((4, NS, B, LANES), F32),
            pltpu.VMEM((NS, 4, B, LANES), F32),
            pltpu.VMEM((4, NS, B, LANES), F32),
            pltpu.VMEM((NS, B, LANES), F32),
            pltpu.VMEM((NS, B, LANES), F32),
            pltpu.VMEM((B, LANES), F32),
            pltpu.VMEM((2, B, LANES), F32),
            pltpu.VMEM((NA, PIECE, LANES), F32),
            pltpu.VMEM((NA, PIECE, LANES), F32),
            dma((40,)), dma((4,)),
            dma((3,)), dma((3,)),
            dma((1,)), dma((1,)),
            dma((NS, 4)), dma((4,)), dma((NS, 4)), dma((4,)),
            dma((1,)), dma((1,)),
            dma((2,)), dma((2,)),
            dma((NC,)), dma((NC,)),
            dma((NA,)), dma((NA,)),
            dma((NC,)), dma((NC,)),
            dma((NC,)), dma((NC,)),
            dma((4,)), dma((2, NC)),
            dma((NC,)), dma((NC,)),
        ],
        compiler_params=pltpu.CompilerParams(has_side_effects=True, collective_id=0),
        name="exchange",
    )(tile_list, tile_valid, inverse_front, factor, unit_lower, pivot_inverse)

    return pl.pallas_call(
        place,
        out_shape=(
            jax.ShapeDtypeStruct((4 * B, NS * W), F32),
            jax.ShapeDtypeStruct((NS, W, W), F32),
        ),
        in_specs=[smem, smem, vmem, vmem],
        out_specs=(hbm, hbm),
        scratch_shapes=[
            pltpu.VMEM((B, W), F32),
            pltpu.VMEM((NS, B, W), F32),
            pltpu.VMEM((NS, W, W), F32),
            dma((NS, 4)),
            dma((4,)),
        ],
        name="place",
    )(
        tile_list,
        tile_valid,
        pltpu.with_memory_space_constraint(c_all, pltpu.VMEM),
        pltpu.with_memory_space_constraint(d_all, pltpu.VMEM),
    )


def solution(mesh):
    in_specs = (P("row", "col"), P("row", None), P(), P(), P(), P())
    out_specs = (P("row", None), P())
    return jax.shard_map(shards, mesh=mesh, in_specs=in_specs, out_specs=out_specs, check_vma=False)
```
